32 devices in a mesh: inline: 2 (over core), tile: 16 (over z, y, x).
Axes of the slice: x: 2, y: 2, z: 4, core: 2. Of those that a mesh axis runs over, the one named last changes fastest.
Arguments:
- features: bfloat16 [96, 4, 32, 128], P(None, 'inline', 'tile'), may hold values from -13 to 13
- conv1_weight: bfloat16 [96, 27, 96], replicated, may hold values from -0.125 to 0.125
- conv2_weight: bfloat16 [96, 27, 96], replicated, may hold values from -0.125 to 0.125
- fault_head: bfloat16 [96, 2], replicated, may hold values from -0.625 to 0.625
- horizon_head: bfloat16 [96, 4], replicated, may hold values from -0.625 to 0.625
- salt_query: bfloat16 [96], replicated, may hold values from -0.625 to 0.625
- salt_head: bfloat16 [96, 2], replicated, may hold values from -0.625 to 0.625
- fault_labels: int32 [4, 32, 128], P('inline', 'tile'), may hold values from 0 to 1
- horizon_labels: int32 [4, 32, 128], P('inline', 'tile'), may hold values from 0 to 3
- salt_labels: int32 [4, 128], P('inline'), may hold values from 0 to 1
Outputs:
- grads: float32 [2, 3, 248832], P(None, None, ('inline', 'tile'))
- gram: float32 [2, 3, 3], replicated
The draws below stay inside these ranges and needn't reach their ends.
All inputs are finite; a program needn't handle non-finite values.
Results may differ from the reference program's by a relative error of at most 0.0043.
Values may be sent and summed in bfloat16 or wider, within the bound.
No kernel may reach another device: no remote copies, remote signals or barrier semaphores. Data moves between devices by JAX's collectives and lax.ppermute only.
A program may use at most 128 MiB of HBM per device.

```python
import math
import jax
import jax.numpy as jnp
from jax import lax

C = 96
FAULT_CLASSES = 2
HORIZON_CLASSES = 4
SALT_CLASSES = 2
D1 = 1
D2 = 2
Y = 128
NX = 4
NZ = 32


def draw_features(key, part):
    chan = 10.0 ** (jnp.arange(C, dtype=jnp.float32) / (C - 1) - 0.5)
    base = jnp.clip(jax.random.normal(key, (C, NX, NZ, Y), jnp.float32), -4.0, 4.0)
    return (base * chan[:, None, None, None]).astype(jnp.bfloat16)


def plant(entries, own_key, smallest, top_value):
    shape = entries.shape
    place = [jax.random.randint(jax.random.fold_in(own_key, axis), (), 0, shape[axis]) for axis in range(len(shape))]
    entries = entries.at[tuple(place)].set(smallest)
    longest = shape.index(max(shape))
    place[longest] = (place[longest] + 1) % shape[longest]
    return entries.at[tuple(place)].set(top_value)


def centred(rng, extent, deviation, reach, kind=jnp.bfloat16):
    return jnp.clip(deviation * jax.random.normal(rng, extent, jnp.float32), -reach, reach).astype(kind)


def setup_inputs(seed: int = 0) -> dict:
    keys = jax.random.split(jax.random.key(seed), 11)
    return {
        "features": draw_features(jax.random.fold_in(keys[10], 71), 0),
        "conv1_weight": centred(keys[1], (C, 27, C), (27 * C) ** -0.5, 0.125),
        "conv2_weight": centred(keys[2], (C, 27, C), (27 * C) ** -0.5, 0.125),
        "fault_head": centred(keys[3], (C, FAULT_CLASSES), C ** -0.5, 0.625),
        "horizon_head": centred(keys[4], (C, HORIZON_CLASSES), C ** -0.5, 0.625),
        "salt_query": centred(keys[5], (C,), C ** -0.5, 0.625),
        "salt_head": centred(keys[6], (C, SALT_CLASSES), C ** -0.5, 0.625),
        "fault_labels": plant(jax.random.randint(keys[7], (NX, NZ, Y), 0, FAULT_CLASSES), jax.random.fold_in(keys[7], 1), 0, FAULT_CLASSES - 1).astype(jnp.int32),
        "horizon_labels": plant(jax.random.randint(keys[8], (NX, NZ, Y), 0, HORIZON_CLASSES), jax.random.fold_in(keys[8], 1), 0, HORIZON_CLASSES - 1).astype(jnp.int32),
        "salt_labels": plant(jax.random.randint(keys[9], (NX, Y), 0, SALT_CLASSES), jax.random.fold_in(keys[9], 1), 0, SALT_CLASSES - 1).astype(jnp.int32),
    }


CAPPING = 8.0
HIGH = lax.Precision.HIGHEST

def capped(value):
    return CAPPING * jnp.tanh(value / CAPPING)

def cap_slope(value):
    squash = jnp.tanh(value / CAPPING)
    return 1.0 - squash * squash

def silu_slope(value):
    sig = jax.nn.sigmoid(value)
    return sig * (1.0 + value * (1.0 - sig))

def dilated_conv(field, weight, dilation):
    chans = weight.shape[0]
    kernel = weight.astype(jnp.float32).reshape(chans, 3, 3, 3, chans).transpose(4, 0, 1, 2, 3)
    return lax.conv_general_dilated(field.astype(jnp.float32), kernel, (1, 1, 1), [(dilation, dilation)] * 3, rhs_dilation=(dilation, dilation, dilation), dimension_numbers=('NCDHW', 'OIDHW', 'NCDHW'), precision=HIGH)

def flipped(weight):
    return weight[:, ::-1, :].transpose(2, 1, 0)

def weight_grad(field, deltas, dilation):
    chans, inline_cells, depth_cells, cross_cells = field.shape
    padded = jnp.pad(field.astype(jnp.float32), ((0, 0), (dilation, dilation), (dilation, dilation), (dilation, dilation)))
    deltas32 = deltas.astype(jnp.float32)

    def one_tap(index):
        along_x = index // 9
        along_z = index // 3 % 3
        along_y = index % 3
        tap = lax.dynamic_slice(padded, (jnp.int32(0), along_x * dilation, along_z * dilation, along_y * dilation), (chans, inline_cells, depth_cells, cross_cells))
        return jnp.einsum('ixzy,toxzy->tio', tap, deltas32, precision=HIGH)
    per_tap = lax.map(one_tap, jnp.arange(27, dtype=jnp.int32))
    return per_tap.transpose(1, 2, 0, 3)

def head_cotangent(second_out, head, labels, scale):
    field = second_out.astype(jnp.float32)
    head32 = head.astype(jnp.float32)
    raw = jnp.einsum('cxzy,cn->nxzy', field, head32, precision=HIGH)
    expo = jnp.exp(capped(raw))
    prob = expo / lax.optimization_barrier(jnp.sum(expo, axis=0, keepdims=True))
    classes = jnp.arange(head.shape[1], dtype=jnp.int32)
    onehot = (labels[None] == classes[:, None, None, None]).astype(jnp.float32)
    dlog = (prob - onehot) * cap_slope(raw) * scale
    return jnp.einsum('cn,nxzy->cxzy', head32, dlog, precision=HIGH)

def trace_backward(field32, raw, expo, num, total, query, head, labels, scale):
    head32 = head.astype(jnp.float32)
    pooled = num / total[None]
    salt_raw = jnp.einsum('cxy,cn->nxy', pooled, head32, precision=HIGH)
    salt_exp = jnp.exp(capped(salt_raw))
    prob = salt_exp / lax.optimization_barrier(jnp.sum(salt_exp, axis=0, keepdims=True))
    classes = jnp.arange(head.shape[1], dtype=jnp.int32)
    onehot = (labels[None] == classes[:, None, None]).astype(jnp.float32)
    dlog = (prob - onehot) * cap_slope(salt_raw) * scale
    dvec = jnp.einsum('cn,nxy->cxy', head32, dlog, precision=HIGH)
    attn = expo / total[:, None, :]
    along = jnp.einsum('cxy,cxzy->xzy', dvec, field32, precision=HIGH)
    inner = lax.optimization_barrier(jnp.sum(dvec * pooled, axis=0))
    dscore = attn * (along - inner[:, None, :]) * cap_slope(raw)
    return attn[None] * dvec[:, :, None, :] + dscore[None] * query.astype(jnp.float32)[:, None, None, None]

def reference(features, conv1_weight, conv2_weight, fault_head, horizon_head, salt_query, salt_head, fault_labels, horizon_labels, salt_labels):
    chans, inline_cells, depth_cells, cross_cells = features.shape
    scale = 1.0 / math.sqrt(inline_cells * depth_cells * cross_cells)
    first_pre = dilated_conv(features[None], conv1_weight, D1)[0]
    first_out = (features.astype(jnp.float32) + jax.nn.silu(first_pre)).astype(jnp.bfloat16)
    second_pre = dilated_conv(first_out[None], conv2_weight, D2)[0]
    second_out = (first_out.astype(jnp.float32) + jax.nn.silu(second_pre)).astype(jnp.bfloat16)
    fault_cot = head_cotangent(second_out, fault_head, fault_labels, scale)
    horizon_cot = head_cotangent(second_out, horizon_head, horizon_labels, scale)
    field32 = second_out.astype(jnp.float32)
    raw = jnp.einsum('cxzy,c->xzy', field32, salt_query.astype(jnp.float32), precision=HIGH)
    expo = jnp.exp(capped(raw))
    total = lax.optimization_barrier(jnp.sum(expo, axis=1))
    num = jnp.einsum('xzy,cxzy->cxy', expo, field32, precision=HIGH)
    salt_cot = trace_backward(field32, raw, expo, num, total, salt_query, salt_head, salt_labels, depth_cells * scale)
    cot = jnp.stack([fault_cot, horizon_cot, salt_cot])
    second_delta = (cot * silu_slope(second_pre)[None]).astype(jnp.bfloat16)
    second_grad = weight_grad(first_out, second_delta, D2)
    first_cot = cot + dilated_conv(second_delta, flipped(conv2_weight), D2)
    first_delta = (first_cot * silu_slope(first_pre)[None]).astype(jnp.bfloat16)
    first_grad = weight_grad(features, first_delta, D1)
    grads = jnp.stack([first_grad.reshape(3, -1), second_grad.reshape(3, -1)])
    gram = jnp.einsum('bti,bui->btu', grads, grads, precision=HIGH) / (27 * C * C)
    return (grads, gram)
```

```python
import math

import jax
import jax.numpy as jnp
from jax import lax
from jax.sharding import PartitionSpec as P

D1 = 1
D2 = 2


CAPPING = 8.0
HIGH = lax.Precision.HIGHEST


def padded_2(x, sides, width):
    for axis, dim in sides:
        count, length = (lax.axis_size(axis), x.shape[dim])
        up = [(i, (i + 1) % count) for i in range(count - 1)]
        down = [(j, i) for i, j in up]
        last = lax.slice_in_dim(x, length - width, length, axis=dim)
        initial = lax.slice_in_dim(x, 0, width, axis=dim)
        before = lax.ppermute(last, axis, up)
        after = lax.ppermute(initial, axis, down)
        x = jnp.concatenate([before, x, after], axis=dim)
    return x


def capped(value):
    return CAPPING * jnp.tanh(value / CAPPING)


def cap_slope(value):
    squash = jnp.tanh(value / CAPPING)
    return 1.0 - squash * squash


def silu_slope(value):
    sig = jax.nn.sigmoid(value)
    return sig * (1.0 + value * (1.0 - sig))


def pad_cross(field, dilation):
    return jnp.pad(field, [(0, 0)] * (field.ndim - 1) + [(dilation, dilation)])


def conv_local(padded, weight, dilation, inline_cells, depth_cells, cross_cells):
    result = None
    for along_x in range(3):
        for along_z in range(3):
            block = padded[
                :,
                :,
                along_x * dilation : along_x * dilation + inline_cells,
                along_z * dilation : along_z * dilation + depth_cells,
                :,
            ]
            taps = jnp.stack(
                [
                    block[..., along_y * dilation : along_y * dilation + cross_cells]
                    for along_y in range(3)
                ],
                axis=2,
            )
            first_tap = (along_x * 3 + along_z) * 3
            kernel = weight[:, first_tap : first_tap + 3, :]
            term = jnp.einsum("ikd,bikxzy->bdxzy", kernel, taps, preferred_element_type=jnp.float32)
            result = term if result is None else result + term
    return result


def weight_local(padded, deltas, dilation, inline_cells, depth_cells, cross_cells):
    pieces = []
    for along_x in range(3):
        for along_z in range(3):
            block = padded[
                :,
                along_x * dilation : along_x * dilation + inline_cells,
                along_z * dilation : along_z * dilation + depth_cells,
                :,
            ]
            taps = jnp.stack(
                [
                    block[..., along_y * dilation : along_y * dilation + cross_cells]
                    for along_y in range(3)
                ],
                axis=1,
            )
            pieces.append(
                jnp.einsum("ikxzy,toxzy->tiko", taps, deltas, preferred_element_type=jnp.float32)
            )
    return jnp.concatenate(pieces, axis=2)


def head_cotangent(second_out, head, labels, scale):
    raw = jnp.einsum("cxzy,cn->nxzy", second_out, head, preferred_element_type=jnp.float32)
    expo = jnp.exp(capped(raw))
    prob = expo / jnp.sum(expo, axis=0, keepdims=True)
    classes = jnp.arange(head.shape[1], dtype=jnp.int32)
    onehot = (labels[None] == classes[:, None, None, None]).astype(jnp.float32)
    dlog = (prob - onehot) * cap_slope(raw) * scale
    return jnp.einsum("cn,nxzy->cxzy", head.astype(jnp.float32), dlog, precision=HIGH)


def bits(count):
    return [1 << bit for bit in range(count.bit_length() - 1)]


def swap_pairs(count, distance):
    return [(i, i ^ distance) for i in range(count)]


def reduce_shares(terms, axes):
    for axis in axes:
        count = lax.axis_size(axis)
        if count & (count - 1):
            return lax.psum_scatter(terms.astype(jnp.float32), axes, scatter_dimension=0)
    rest = terms.shape[1:]
    order = [(axis, distance) for axis in axes for distance in bits(lax.axis_size(axis))]
    left = [(axis, distance) for axis in axes for distance in reversed(bits(lax.axis_size(axis)))]
    terms = terms.reshape((2,) * len(left) + rest)
    for axis, distance in order:
        place = left.index((axis, distance))
        left.pop(place)
        bit = (lax.axis_index(axis) // distance) % 2
        kept = lax.dynamic_index_in_dim(terms, bit, place, False)
        given = lax.dynamic_index_in_dim(terms, 1 - bit, place, False)
        taken = lax.ppermute(given, axis, swap_pairs(lax.axis_size(axis), distance))
        terms = kept.astype(jnp.float32) + taken.astype(jnp.float32)
        if left:
            terms = terms.astype(jnp.bfloat16)
    return terms


def sum_all(value, axes):
    for axis in axes:
        count = lax.axis_size(axis)
        if count & (count - 1):
            value = lax.psum(value, axis)
            continue
        for distance in bits(count):
            value = value + lax.ppermute(value, axis, swap_pairs(count, distance))
    return value


def trace_terms(field, query, head):
    raw = jnp.einsum("cxzy,c->xzy", field, query, preferred_element_type=jnp.float32)
    part = jnp.einsum("cxzy,cn->nxzy", field, head, preferred_element_type=jnp.float32)
    expo = jnp.exp(capped(raw))
    sums = jnp.concatenate([jnp.sum(expo, axis=1)[None], jnp.sum(expo[None] * part, axis=2)])
    return (raw, part, expo, sums)


def trace_backward(raw, part, expo, sums, query, head, labels, scale):
    total = sums[0]
    salt_raw = sums[1:] / total[None]
    salt_exp = jnp.exp(capped(salt_raw))
    prob = salt_exp / jnp.sum(salt_exp, axis=0, keepdims=True)
    classes = jnp.arange(head.shape[1], dtype=jnp.int32)
    onehot = (labels[None] == classes[:, None, None]).astype(jnp.float32)
    dlog = (prob - onehot) * cap_slope(salt_raw) * scale
    attn = expo / total[:, None, :]
    along = jnp.sum(dlog[:, :, None, :] * part, axis=0)
    inner = jnp.sum(dlog * salt_raw, axis=0)
    dscore = attn * (along - inner[:, None, :]) * cap_slope(raw)
    rows = jnp.concatenate([attn[None] * dlog[:, :, None, :], dscore[None]])
    columns = jnp.concatenate([head, query[:, None]], axis=1).astype(jnp.float32)
    return jnp.einsum("cn,nxzy->cxzy", columns, rows, precision=HIGH)


def on_device(
    features,
    conv1_weight,
    conv2_weight,
    fault_head,
    horizon_head,
    salt_query,
    salt_head,
    fault_labels,
    horizon_labels,
    salt_labels,
):
    chans, inline_cells, depth_cells, cross_cells = features.shape
    tile_count = lax.axis_size("tile")
    depth_total = depth_cells * tile_count
    scale = 1.0 / math.sqrt(inline_cells * lax.axis_size("inline") * depth_total * cross_cells)
    input_pad = pad_cross(padded_2(features, (("inline", 1), ("tile", 2)), D1), D1)
    first_pre = conv_local(
        input_pad[None], conv1_weight, D1, inline_cells, depth_cells, cross_cells
    )[0]
    first_out = (features.astype(jnp.float32) + jax.nn.silu(first_pre)).astype(jnp.bfloat16)
    hidden_pad = pad_cross(padded_2(first_out, (("inline", 1), ("tile", 2)), D2), D2)
    second_pre = conv_local(
        hidden_pad[None], conv2_weight, D2, inline_cells, depth_cells, cross_cells
    )[0]
    second_out = (first_out.astype(jnp.float32) + jax.nn.silu(second_pre)).astype(jnp.bfloat16)
    fault_cot = head_cotangent(second_out, fault_head, fault_labels, scale)
    horizon_cot = head_cotangent(second_out, horizon_head, horizon_labels, scale)
    raw, part, expo, sums = trace_terms(second_out, salt_query, salt_head)
    sums = sum_all(sums, ("tile",))
    salt_cot = trace_backward(
        raw, part, expo, sums, salt_query, salt_head, salt_labels, depth_total * scale
    )
    cot = jnp.stack([fault_cot, horizon_cot, salt_cot])
    second_delta = (cot * silu_slope(second_pre)[None]).astype(jnp.bfloat16)
    second_grad = weight_local(hidden_pad, second_delta, D2, inline_cells, depth_cells, cross_cells)
    delta_pad = pad_cross(padded_2(second_delta, (("inline", 2), ("tile", 3)), D2), D2)
    turned = conv2_weight[:, ::-1, :].transpose(2, 1, 0)
    first_cot = cot + conv_local(delta_pad, turned, D2, inline_cells, depth_cells, cross_cells)
    first_delta = (first_cot * silu_slope(first_pre)[None]).astype(jnp.bfloat16)
    first_grad = weight_local(input_pad, first_delta, D1, inline_cells, depth_cells, cross_cells)
    axes = ("inline", "tile")
    device_count = lax.axis_size(axes)
    norm_count = 27 * chans * chans
    terms = jnp.stack([first_grad, second_grad]).astype(jnp.bfloat16)
    terms = terms.reshape(2, 3, device_count, -1).transpose(2, 0, 1, 3)
    grads = reduce_shares(terms, axes)
    gram = jnp.sum(grads[:, :, None, :] * grads[:, None, :, :], axis=3)
    gram = sum_all(gram, axes) / norm_count
    return (grads, gram)


def solution(mesh):
    in_specs = (
        P(None, "inline", "tile", None),
        P(),
        P(),
        P(),
        P(),
        P(),
        P(),
        P("inline", "tile", None),
        P("inline", "tile", None),
        P("inline", None),
    )
    out_specs = (P(None, None, ("inline", "tile")), P())
    return jax.shard_map(
        on_device, mesh=mesh, in_specs=in_specs, out_specs=out_specs, check_vma=False
    )
```

```python
import functools
import math

import jax
import jax.numpy as jnp
from jax import lax
from jax.experimental import pallas as pl
from jax.experimental.pallas import tpu as pltpu
from jax.sharding import PartitionSpec as P

D1 = 1
D2 = 2
REACH = D1 + 2 * D2

CAPPING = 8.0
LABEL_ROWS = 8
AXES = ("inline", "tile")


def round_up(value, unit):
    return -(-value // unit) * unit


def bits(count):
    return [1 << bit for bit in range(count.bit_length() - 1)]


def swap_pairs(count, distance):
    return [(i, i ^ distance) for i in range(count)]


def window(cells, axis, dim, halo):
    count, length = (lax.axis_size(axis), cells.shape[dim])
    covered, hops = (0, 1)
    while covered < halo:
        amount = min(halo - covered, length + covered)
        size = cells.shape[dim]
        start = lax.slice_in_dim(cells, covered, covered + amount, axis=dim)
        end = lax.slice_in_dim(cells, size - covered - amount, size - covered, axis=dim)
        up = [(i, i + hops) for i in range(count - hops)]
        down = [(j, i) for i, j in up]
        before = lax.ppermute(end, axis, up)
        after = lax.ppermute(start, axis, down)
        cells = jnp.concatenate([before, cells, after], axis=dim)
        covered += amount
        hops = covered // length + 1
    return cells


def ring(cells, axis, dim):
    count = lax.axis_size(axis)
    blocks = [cells]
    for hop in range(1, count):
        pairs = [((i + hop) % count, i) for i in range(count)]
        blocks.append(lax.ppermute(cells, axis, pairs))
    return jnp.concatenate(blocks, axis=dim)


def sum_all(value, axes):
    for axis in axes:
        for distance in bits(lax.axis_size(axis)):
            pairs = swap_pairs(lax.axis_size(axis), distance)
            value = value + lax.ppermute(value, axis, pairs)
    return value


def halving_order(axes):
    return [(axis, distance) for axis in axes for distance in bits(lax.axis_size(axis))]


def reduce_shares(kept, given, left, order):
    for step, (axis, distance) in enumerate(order):
        place = left.index((axis, distance))
        bit = (lax.axis_index(axis) // distance) % 2
        if step or given is None:
            given = lax.dynamic_index_in_dim(kept, 1 - bit, place, False).astype(jnp.bfloat16)
            kept = lax.dynamic_index_in_dim(kept, bit, place, False)
        left = left[:place] + left[place + 1 :]
        taken = lax.ppermute(given, axis, swap_pairs(lax.axis_size(axis), distance))
        kept = kept + taken.astype(jnp.float32)
    return kept


class Plan:
    def __init__(self, inline_count, tile_count, inline_cells, depth_cells, chans, shares):
        self.inline_count, self.inline_cells = (inline_count, inline_cells)
        self.depth_cells = depth_cells
        self.inline_total = inline_count * inline_cells
        self.depth_total = tile_count * depth_cells
        self.chans = chans
        self.whole = (
            self.inline_total <= inline_cells + 2 * REACH and depth_cells % inline_count == 0
        )
        self.own_depth = depth_cells // inline_count if self.whole else depth_cells
        own = range(self.own_depth)
        spread = lambda cells, d: sorted({z + d * b for z in cells for b in (-1, 0, 1)})
        self.z = {"own": list(own)}
        self.z["second"] = spread(self.z["own"], D2)
        self.z["first"] = spread(self.z["second"], D2)
        self.z["input"] = spread(self.z["first"], D1)
        self.z["near1"] = spread(self.z["own"], D1)
        self.z["near2"] = self.z["second"]
        self.z["middle"] = self.z["own"]
        reach = {"own": 0, "second": D2, "first": 2 * D2, "input": REACH, "near1": D1, "near2": D2}
        reach["middle"] = D2
        self.x = {}
        for name, halo in reach.items():
            if self.whole:
                self.x[name] = (0, self.inline_total)
            else:
                self.x[name] = (-halo, inline_cells + halo)
        self.aligned = chans % shares == 0
        self.groups = shares if self.aligned else chans
        self.per_group = chans // self.groups
        self.pitch = round_up(27 * self.per_group, 8)

    def planes(self, name):
        low, high = self.x[name]
        return (high - low) * len(self.z[name])

    def index(self, name, x, z):
        return (x - self.x[name][0]) * len(self.z[name]) + self.z[name].index(z)

    def runs(self, name, step):
        low, high = self.x[name]
        found = []
        for x in range(low, high):
            if self.whole:
                taps = tuple(a for a in (-1, 0, 1) if 0 <= x + step * a < self.inline_total)
            else:
                taps = (-1, 0, 1)
            if found and found[-1][0] == taps:
                found[-1][2] += 1
            else:
                found.append([taps, x, 1])
        return found


def depth_base(plan):
    start = lax.axis_index("tile") * plan.depth_cells
    if plan.whole:
        start = start + lax.axis_index("inline") * plan.own_depth
    return start


def inside(plan, x, z):
    depth = depth_base(plan) + z
    good = (depth >= 0) & (depth < plan.depth_total)
    if not plan.whole:
        cell = lax.axis_index("inline") * plan.inline_cells + x
        good = good & (cell >= 0) & (cell < plan.inline_total)
    return good


def source_index(plan, x, z):
    depth_width = plan.depth_cells + 2 * REACH
    if not plan.whole:
        return (x + REACH) * depth_width + z + REACH
    here = lax.axis_index("inline")
    block = lax.rem(x // plan.inline_cells + plan.inline_count - here, plan.inline_count)
    column = block * plan.inline_cells + lax.rem(x, plan.inline_cells)
    return column * depth_width + z + REACH + here * plan.own_depth


def each(count, body):
    if count == 1:
        body(0)
    else:
        lax.fori_loop(0, count, lambda i, carry: (body(i), carry)[1], 0)


def shifted(plane, amount):
    if amount == 0:
        return plane
    width = plane.shape[1]
    column = lax.broadcasted_iota(jnp.int32, plane.shape, 1) + amount
    rolled = pltpu.roll(plane, (-amount) % width, 1)
    return jnp.where((column >= 0) & (column < width), rolled, 0.0)


def store_taps(ref, index, plane, offsets):
    chans = plane.shape[0]
    for place, amount in enumerate(offsets):
        ref[index, place * chans : (place + 1) * chans, :] = shifted(plane, amount).astype(
            jnp.bfloat16
        )


def sigmoid(value):
    return 1.0 / (1.0 + jnp.exp(-value))


def slope_of(value, sig):
    return sig * (1.0 + value * (1.0 - sig))


def matmul(left, right):
    return lax.dot_general(
        left, right, (((1,), (0,)), ((), ())), preferred_element_type=jnp.float32
    )


def matmul_nt(left, right):
    return lax.dot_general(
        left, right, (((1,), (1,)), ((), ())), preferred_element_type=jnp.float32
    )


def conv(weight_ref, taps, columns):
    total = None
    for a in taps:
        term = matmul(weight_ref[a + 1], columns(a))
        total = term if total is None else total + term
    return total


def joined(pieces, axis):
    return pieces[0] if len(pieces) == 1 else jnp.concatenate(pieces, axis=axis)


def softmax_cot(raw, expo, slope, label, scale):
    count = len(raw)
    total = expo[0]
    for n in range(1, count):
        total = total + expo[n]
    found = []
    for n in range(count):
        hit = jnp.where(label == float(n), 1.0, 0.0)
        found.append((expo[n] / total - hit) * slope[n] * scale)
    return found


def forward_kernel(
    plan,
    classes,
    scale,
    planes_ref,
    w1_ref,
    w2_ref,
    rows_ref,
    cols_ref,
    near1_ref,
    near2_ref,
    slope1_ref,
    slope2_ref,
    delta_ref,
    cot_ref,
    stats_ref,
    sums_ref,
    input_ref,
    first_ref,
    base_ref,
):
    chans = plan.chans
    faults, horizons, salts = classes
    zs = plan.z

    low, high = plan.x["input"]

    def load(i):
        x = low + i
        for z in zs["input"]:
            plane = planes_ref[source_index(plan, x, z), :chans, :].astype(jnp.float32)
            store_taps(input_ref, plan.index("input", x, z), plane, (-D1, 0, D1))

    each(high - low, load)

    for taps, begin, count in plan.runs("first", D1):

        def first(i, taps=taps, begin=begin):
            x = begin + i

            def columns(a):
                return joined(
                    [
                        joined(
                            [
                                input_ref[plan.index("input", x + D1 * a, z + D1 * b)]
                                for b in (-1, 0, 1)
                            ],
                            0,
                        )
                        for z in zs["first"]
                    ],
                    1,
                )

            pre = conv(w1_ref, taps, columns)
            for j, z in enumerate(zs["first"]):
                value = pre[:, j * 128 : (j + 1) * 128]
                field = input_ref[plan.index("input", x, z), chans : 2 * chans, :]
                sig = sigmoid(value)
                out = field.astype(jnp.float32) + value * sig
                out = out.astype(jnp.bfloat16).astype(jnp.float32)
                out = jnp.where(inside(plan, x, z), out, 0.0)
                store_taps(first_ref, plan.index("first", x, z), out, (-D2, 0, D2))
                if z in zs["own"]:
                    base_ref[plan.index("first", x, z)] = slope_of(value, sig)

        each(count, first)

    own_low, own_high = plan.x["own"]

    def keep_slope(i):
        x = own_low + i
        for z in zs["own"]:
            slope1_ref[plan.index("own", x, z)] = base_ref[plan.index("first", x, z)]

    each(own_high - own_low, keep_slope)

    for name, ref, source, source_ref in (
        ("near1", near1_ref, "input", input_ref),
        ("near2", near2_ref, "first", first_ref),
    ):
        near_low, near_high = plan.x[name]

        def keep(i, name=name, ref=ref, source=source, source_ref=source_ref, near_low=near_low):
            x = near_low + i
            for z in zs[name]:
                ref[plan.index(name, x, z)] = source_ref[plan.index(source, x, z)]

        each(near_high - near_low, keep)

    spread = [
        jnp.broadcast_to(cols_ref[:, n : n + 1], (chans, 128)) for n in range(faults + horizons)
    ]
    for n in range(faults + horizons):
        base_ref[n] = spread[n]

    for taps, begin, count in plan.runs("second", D2):

        def second(i, taps=taps, begin=begin):
            x = begin + i

            def columns(a):
                return joined(
                    [
                        joined(
                            [
                                first_ref[plan.index("first", x + D2 * a, z + D2 * b)]
                                for b in (-1, 0, 1)
                            ],
                            0,
                        )
                        for z in zs["second"]
                    ],
                    1,
                )

            pre = conv(w2_ref, taps, columns)
            field = joined(
                [
                    first_ref[plan.index("first", x, z), chans : 2 * chans, :]
                    for z in zs["second"]
                ],
                1,
            )
            sig = sigmoid(pre)
            slope2 = slope_of(pre, sig)
            second_out = (field.astype(jnp.float32) + pre * sig).astype(jnp.bfloat16)
            raw = matmul(rows_ref[...], second_out)
            squash = jnp.tanh(raw / CAPPING)
            expo = jnp.exp(CAPPING * squash)
            slope = 1.0 - squash * squash
            sums = None
            for j, z in enumerate(zs["second"]):
                lanes = slice(j * 128, (j + 1) * 128)
                row = lambda table, n: table[n : n + 1, lanes]
                marks = planes_ref[source_index(plan, x, z), chans : chans + LABEL_ROWS, :].astype(
                    jnp.float32
                )
                good = inside(plan, x, z)
                here = plan.index("second", x, z)
                slope2_ref[here] = slope2[:, lanes]
                for task, start, size in ((0, 0, faults), (1, faults, horizons)):
                    span = range(start, start + size)
                    dlog = softmax_cot(
                        [row(raw, n) for n in span],
                        [row(expo, n) for n in span],
                        [row(slope, n) for n in span],
                        marks[task : task + 1, :],
                        scale,
                    )
                    cot = None
                    for n, factor in zip(span, dlog):
                        term = base_ref[n] * factor
                        cot = term if cot is None else cot + term
                    if z in zs["own"]:
                        cot_ref[task, plan.index("middle", x, z)] = cot
                    delta = jnp.where(good, cot * slope2[:, lanes], 0.0)
                    delta_ref[task, here] = delta.astype(jnp.bfloat16)
                query = faults + horizons
                pieces = [row(expo, query)]
                pieces += [row(raw, query + 1 + n) for n in range(salts)]
                pieces += [row(slope, query), marks[2:3, :]]
                for n, piece in enumerate(pieces):
                    stats_ref[here, n : n + 1, :] = piece
                if z in zs["own"]:
                    terms = [pieces[0]] + [pieces[0] * piece for piece in pieces[1 : 1 + salts]]
                    if sums is None:
                        sums = terms
                    else:
                        sums = [old + new for old, new in zip(sums, terms)]
            place = x - plan.x["second"][0]
            sums_ref[place] = jnp.zeros(sums_ref.shape[1:], jnp.float32)
            for n, piece in enumerate(sums):
                sums_ref[place, n : n + 1, :] = piece

        each(count, second)


def salt_cotangents(plan, classes, scale, stats_ref, sums_ref, cols_ref, slope2_ref, delta_ref, cot_ref, spread_ref):
    faults, horizons, salts = classes
    chans = plan.chans
    query = faults + horizons
    for n in range(salts + 1):
        spread_ref[n] = jnp.broadcast_to(cols_ref[:, query + n : query + n + 1], (chans, 128))
    low, high = plan.x["second"]

    def one(i):
        x = low + i
        total = sums_ref[i, 0:1, :]
        salt_raw = [sums_ref[i, 1 + n : 2 + n, :] / total for n in range(salts)]
        squash = [jnp.tanh(value / CAPPING) for value in salt_raw]
        label = stats_ref[plan.index("second", x, 0), salts + 2 : salts + 3, :]
        dlog = softmax_cot(
            salt_raw,
            [jnp.exp(CAPPING * value) for value in squash],
            [1.0 - value * value for value in squash],
            label,
            scale,
        )
        inner = dlog[0] * salt_raw[0]
        for n in range(1, salts):
            inner = inner + dlog[n] * salt_raw[n]
        for z in plan.z["second"]:
            here = plan.index("second", x, z)
            attn = stats_ref[here, 0:1, :] / total
            along = dlog[0] * stats_ref[here, 1:2, :]
            for n in range(1, salts):
                along = along + dlog[n] * stats_ref[here, 1 + n : 2 + n, :]
            dscore = attn * (along - inner) * stats_ref[here, salts + 1 : salts + 2, :]
            cot = spread_ref[0] * dscore
            for n in range(salts):
                cot = cot + spread_ref[1 + n] * (attn * dlog[n])
            cot_ref[0, here] = cot
            delta = jnp.where(inside(plan, x, z), cot * slope2_ref[here], 0.0)
            delta_ref[0, here] = delta.astype(jnp.bfloat16)

    each(high - low, one)


def backward_body(
    plan,
    tasks,
    delta_ref,
    cot_of,
    slope1_ref,
    near1_ref,
    near2_ref,
    w2t_ref,
    order_ref,
    outs,
    taps_ref,
    first_delta_ref,
    second_delta_ref,
    sorted1_ref,
    sorted2_ref,
    rows_refs,
):
    chans, zs = (plan.chans, plan.z)
    width = tasks * chans

    def spread(i):
        for task in range(tasks):
            plane = delta_ref[task, i].astype(jnp.float32)
            store_taps(taps_ref, task * plan.planes("second") + i, plane, (D2, 0, -D2))

    each(plan.planes("second"), spread)

    for ref, target_ref, name in (
        (near1_ref, sorted1_ref, "near1"),
        (near2_ref, sorted2_ref, "near2"),
    ):

        def resort(i, ref=ref, target_ref=target_ref):
            stack = joined([ref[i, c * chans : (c + 1) * chans, :] for c in range(3)], 1)
            stack = matmul(order_ref[...], stack).astype(jnp.bfloat16)
            for c in range(3):
                target_ref[i, c * chans : (c + 1) * chans, :] = stack[:, c * 128 : (c + 1) * 128]

        each(plan.planes(name), resort)

    for taps, begin, count in plan.runs("own", -D2):

        def back(i, taps=taps, begin=begin):
            x = begin + i

            def columns(a):
                return joined(
                    [
                        joined(
                            [
                                taps_ref[
                                    task * plan.planes("second")
                                    + plan.index("second", x - D2 * a, z - D2 * b)
                                ]
                                for b in (-1, 0, 1)
                            ],
                            0,
                        )
                        for task in range(tasks)
                        for z in zs["own"]
                    ],
                    1,
                )

            pulled = conv(w2t_ref, taps, columns)
            column = 0
            for task in range(tasks):
                for z in zs["own"]:
                    here = plan.index("own", x, z)
                    cot = cot_of(task, x, z) + pulled[:, column * 128 : (column + 1) * 128]
                    place = slice(task * chans, (task + 1) * chans)
                    first_delta_ref[here, place, :] = (cot * slope1_ref[here]).astype(jnp.bfloat16)
                    second_delta_ref[here, place, :] = delta_ref[task, plan.index("second", x, z)]
                    column += 1

        each(count, back)

    own_low, own_high = plan.x["own"]
    lanes = 128
    for n in range(plan.pitch - 27 * plan.per_group):
        for ref in rows_refs:
            start = 27 * plan.per_group + n
            ref[pl.ds(start, plan.groups, stride=plan.pitch), :] = jnp.zeros(
                (plan.groups, lanes), jnp.float32
            )
    lead = width % lanes
    for a in (-1, 0, 1):
        for b in (-1, 0, 1):
            chunks = {}
            for ref, name, d, delta_own, begin in (
                (sorted1_ref, "near1", D1, first_delta_ref, 0),
                (sorted2_ref, "near2", D2, second_delta_ref, width),
            ):
                cells = []
                for x in range(own_low, own_high):
                    if plan.whole and not 0 <= x + d * a < plan.inline_total:
                        continue
                    cells += [(x, z) for z in zs["own"]]
                left = joined([ref[plan.index(name, x + d * a, z + d * b)] for x, z in cells], 1)
                right = joined([delta_own[plan.index("own", x, z)] for x, z in cells], 1)
                before = begin % lanes
                after = -(before + width) % lanes
                parts = [right]
                if before:
                    parts = [jnp.zeros((before, right.shape[1]), right.dtype)] + parts
                if after:
                    parts = parts + [jnp.zeros((after, right.shape[1]), right.dtype)]
                grad = matmul_nt(left, joined(parts, 0))
                for n in range(grad.shape[1] // lanes):
                    chunk = begin // lanes + n
                    piece = grad[:, n * lanes : (n + 1) * lanes]
                    chunks[chunk] = chunks[chunk] + piece if chunk in chunks else piece
            for chunk, value in chunks.items():
                for c in range(3):
                    tap = 9 * (a + 1) + 3 * (b + 1) + c
                    for rest in range(plan.per_group):
                        at = c * chans + rest * plan.groups
                        rows_refs[chunk][
                            pl.ds(rest * 27 + tap, plan.groups, stride=plan.pitch), :
                        ] = value[at : at + plan.groups, :]
    if plan.aligned:
        kept_ref, given_ref = outs
        half = lax.rem(lax.axis_index("inline"), 2)
        tiles = plan.groups // plan.inline_count
        for high in range(plan.inline_count // 2):

            def write(j, high=high):
                for chunk, ref in enumerate(rows_refs):
                    span = slice(chunk * lanes, (chunk + 1) * lanes)
                    for target_ref, bit in ((kept_ref, half), (given_ref, 1 - half)):
                        group = (2 * high + bit) * tiles + j
                        start = pl.multiple_of(group * plan.pitch, 8)
                        value = ref[pl.ds(start, plan.pitch), :]
                        target_ref[high * tiles + j, :, span] = value.astype(target_ref.dtype)

            each(tiles, write)
    else:
        (out_ref,) = outs

        def write(j):
            for chunk, ref in enumerate(rows_refs):
                start = pl.multiple_of(j * plan.pitch, 8)
                span = slice(chunk * lanes, (chunk + 1) * lanes)
                out_ref[j, :, span] = ref[pl.ds(start, plan.pitch), :]

        each(plan.groups, write)


def pair_kernel(plan, delta_ref, cot_ref, slope1_ref, near1_ref, near2_ref, w2t_ref, order_ref, *rest):
    outs, scratch = split_refs(plan, rest)
    cot_of = lambda task, x, z: cot_ref[task, plan.index("middle", x, z)]
    backward_body(
        plan, 2, delta_ref, cot_of, slope1_ref, near1_ref, near2_ref, w2t_ref, order_ref, outs,
        *scratch[:5], scratch[5:],
    )


def salt_kernel(
    plan, classes, scale, stats_ref, sums_ref, cols_ref, slope2_ref, slope1_ref, near1_ref, near2_ref,
    w2t_ref, order_ref, *rest
):
    outs, scratch = split_refs(plan, rest)
    delta_ref, cot_ref, spread_ref = scratch[:3]
    salt_cotangents(
        plan, classes, scale, stats_ref, sums_ref, cols_ref, slope2_ref, delta_ref, cot_ref, spread_ref
    )
    cot_of = lambda task, x, z: cot_ref[task, plan.index("second", x, z)]
    scratch = scratch[3:]
    backward_body(
        plan, 1, delta_ref, cot_of, slope1_ref, near1_ref, near2_ref, w2t_ref, order_ref, outs,
        *scratch[:5], scratch[5:],
    )


def split_refs(plan, refs):
    count = 2 if plan.aligned else 1
    return (refs[:count], refs[count:])


def vmem(count):
    return [pl.BlockSpec(memory_space=pltpu.VMEM)] * count


def backward_shapes(plan, tasks):
    chans = plan.chans
    width = round_up(2 * tasks * chans, 128)
    if plan.aligned:
        shape = (plan.groups // 2, plan.pitch, width)
        outs = [jax.ShapeDtypeStruct(shape, jnp.float32), jax.ShapeDtypeStruct(shape, jnp.bfloat16)]
    else:
        outs = [jax.ShapeDtypeStruct((plan.groups, plan.pitch, width), jnp.float32)]
    scratch = [
        pltpu.VMEM((tasks * plan.planes("second"), 3 * chans, 128), jnp.bfloat16),
        pltpu.VMEM((plan.planes("own"), tasks * chans, 128), jnp.bfloat16),
        pltpu.VMEM((plan.planes("own"), tasks * chans, 128), jnp.bfloat16),
        pltpu.VMEM((plan.planes("near1"), 3 * chans, 128), jnp.bfloat16),
        pltpu.VMEM((plan.planes("near2"), 3 * chans, 128), jnp.bfloat16),
    ]
    scratch += [pltpu.VMEM((plan.groups * plan.pitch, 128), jnp.float32)] * (width // 128)
    return (outs, scratch)


def tap_major(weight, flip):
    ins, _, outs = weight.shape
    parts = weight.reshape(ins, 3, 9, outs)
    if flip:
        return parts.transpose(1, 0, 2, 3).reshape(3, ins, 9 * outs)
    return parts.transpose(1, 3, 2, 0).reshape(3, outs, 9 * ins)


def on_device(
    features,
    conv1_weight,
    conv2_weight,
    fault_head,
    horizon_head,
    salt_query,
    salt_head,
    fault_labels,
    horizon_labels,
    salt_labels,
):
    chans, inline_cells, depth_cells, cross_cells = features.shape
    inline_count, tile_count = (lax.axis_size("inline"), lax.axis_size("tile"))
    shares = inline_count * tile_count
    plan = Plan(inline_count, tile_count, inline_cells, depth_cells, chans, shares)
    scale = 1.0 / math.sqrt(plan.inline_total * plan.depth_total * cross_cells)
    classes = (fault_head.shape[1], horizon_head.shape[1], salt_head.shape[1])

    marks = jnp.stack(
        [
            fault_labels,
            horizon_labels,
            jnp.broadcast_to(salt_labels[:, None, :], fault_labels.shape),
        ],
        axis=2,
    ).astype(jnp.bfloat16)
    marks = jnp.pad(marks, ((0, 0), (0, 0), (0, LABEL_ROWS - 3), (0, 0)))
    planes = jnp.concatenate([features.transpose(1, 2, 0, 3), marks], axis=2)
    planes = window(planes, "tile", 1, REACH)
    if plan.whole:
        planes = ring(planes, "inline", 0)
    else:
        planes = window(planes, "inline", 0, REACH)
    planes = planes.reshape((-1,) + planes.shape[2:])

    cols = jnp.concatenate([fault_head, horizon_head, salt_query[:, None], salt_head], axis=1)
    cols = jnp.pad(cols, ((0, 0), (0, 16 - cols.shape[1])))
    rows = cols.T
    cols = cols.astype(jnp.float32)
    w1 = tap_major(conv1_weight, False)
    w2 = tap_major(conv2_weight, False)
    w2t = tap_major(conv2_weight, True)
    spot = jnp.arange(chans)
    origin = plan.per_group * (spot % plan.groups) + spot // plan.groups
    order = (origin[:, None] == spot[None, :]).astype(jnp.bfloat16)

    f32, bf16 = (jnp.float32, jnp.bfloat16)
    own, second = (plan.planes("own"), plan.planes("second"))
    second_x = plan.x["second"][1] - plan.x["second"][0]
    shape = jax.ShapeDtypeStruct
    near1, near2, slope1, slope2, delta, cot, stats, sums = pl.pallas_call(
        functools.partial(forward_kernel, plan, classes, scale),
        out_shape=[
            shape((plan.planes("near1"), 3 * chans, 128), bf16),
            shape((plan.planes("near2"), 3 * chans, 128), bf16),
            shape((own, chans, 128), f32),
            shape((second, chans, 128), f32),
            shape((2, second, chans, 128), bf16),
            shape((2, plan.planes("middle"), chans, 128), f32),
            shape((second, 8, 128), f32),
            shape((second_x, 8, 128), f32),
        ],
        in_specs=vmem(5),
        out_specs=vmem(8),
        scratch_shapes=[
            pltpu.VMEM((plan.planes("input"), 3 * chans, 128), bf16),
            pltpu.VMEM((plan.planes("first"), 3 * chans, 128), bf16),
            pltpu.VMEM((plan.planes("first"), chans, 128), f32),
        ],
        name="forward",
    )(planes, w1, w2, rows, cols)

    sums = sum_all(sums, AXES if plan.whole else ("tile",))

    outs, scratch = backward_shapes(plan, 2)
    pair = pl.pallas_call(
        functools.partial(pair_kernel, plan),
        out_shape=outs,
        in_specs=vmem(7),
        out_specs=vmem(len(outs)),
        scratch_shapes=scratch,
        name="pair",
    )(delta, cot, slope1, near1, near2, w2t, order)
    outs, scratch = backward_shapes(plan, 1)
    scratch = [
        pltpu.VMEM((1, second, chans, 128), bf16),
        pltpu.VMEM((1, second, chans, 128), f32),
        pltpu.VMEM((1 + classes[2], chans, 128), f32),
    ] + scratch
    salt = pl.pallas_call(
        functools.partial(salt_kernel, plan, classes, plan.depth_total * scale),
        out_shape=outs,
        in_specs=vmem(9),
        out_specs=vmem(len(outs)),
        scratch_shapes=scratch,
        name="salt",
    )(stats, sums, cols, slope2, slope1, near1, near2, w2t, order)

    order1 = halving_order(AXES)
    left = [(axis, d) for axis in AXES for d in reversed(bits(lax.axis_size(axis)))]
    terms = []
    if plan.aligned:
        after = [entry for entry in left if entry != order1[0]]
        for (kept, given), tasks in ((pair, 2), (salt, 1)):
            kept = kept.reshape((2,) * len(after) + kept.shape[1:])
            given = given.reshape(kept.shape)
            share = reduce_shares(kept, given, [order1[0]] + after, order1)
            share = share[: 27 * plan.per_group, : 2 * tasks * chans]
            share = share.reshape(-1, 2, tasks, chans).transpose(1, 2, 0, 3)
            terms.append(share.reshape(2, tasks, -1))
        grads = jnp.concatenate(terms, axis=1)
    else:
        for (value,), tasks in ((pair, 2), (salt, 1)):
            value = value[:, :27, : 2 * tasks * chans].reshape(chans, 27, 2, tasks, chans)
            terms.append(value.transpose(2, 3, 0, 1, 4).reshape(2, tasks, shares, -1))
        flat = jnp.concatenate(terms, axis=1).transpose(2, 0, 1, 3)
        flat = flat.reshape((2,) * len(left) + flat.shape[1:])
        grads = reduce_shares(flat, None, left, order1)
    gram = jnp.sum(grads[:, :, None, :] * grads[:, None, :, :], axis=3)
    gram = sum_all(gram, AXES) / (27 * chans * chans)
    return (grads, gram)


def solution(mesh):
    in_specs = (
        P(None, "inline", "tile", None),
        P(),
        P(),
        P(),
        P(),
        P(),
        P(),
        P("inline", "tile", None),
        P("inline", "tile", None),
        P("inline", None),
    )
    out_specs = (P(None, None, ("inline", "tile")), P())
    return jax.shard_map(
        on_device, mesh=mesh, in_specs=in_specs, out_specs=out_specs, check_vma=False
    )
```

```python
import functools
import math

import jax
import jax.numpy as jnp
from jax import lax
from jax.experimental import pallas as pl
from jax.experimental.pallas import tpu as pltpu
from jax.sharding import PartitionSpec as P

D1 = 1
D2 = 2
REACH = D1 + 2 * D2

CAPPING = 8.0
LABEL_ROWS = 8
AXES = ("inline", "tile")


def round_up(value, unit):
    return -(-value // unit) * unit


def bits(count):
    return [1 << bit for bit in range(count.bit_length() - 1)]


def swap_pairs(count, distance):
    return [(i, i ^ distance) for i in range(count)]


def window(cells, axis, dim, halo):
    count, length = (lax.axis_size(axis), cells.shape[dim])
    covered, hops = (0, 1)
    while covered < halo:
        amount = min(halo - covered, length + covered)
        size = cells.shape[dim]
        start = lax.slice_in_dim(cells, covered, covered + amount, axis=dim)
        end = lax.slice_in_dim(cells, size - covered - amount, size - covered, axis=dim)
        up = [(i, i + hops) for i in range(count - hops)]
        down = [(j, i) for i, j in up]
        before = lax.ppermute(end, axis, up)
        after = lax.ppermute(start, axis, down)
        cells = jnp.concatenate([before, cells, after], axis=dim)
        covered += amount
        hops = covered // length + 1
    return cells


def outward(cells, halo, riders):
    here, length = (lax.axis_index("inline"), cells.shape[1])
    count = lax.axis_size("tile")
    chain = jnp.where(here == 0, cells[:, ::-1], cells)
    side = None
    covered, hops = (0, 1)
    while covered < halo:
        amount = min(halo - covered, length + covered)
        pairs = [(i, i + hops) for i in range(count - hops)]
        pairs += [(count + j, count + i) for i, j in pairs]
        taken = lax.ppermute(chain[:, :amount], AXES, pairs)
        if side is None:
            taken, *riders = lax.optimization_barrier((taken, *riders))
        side = taken if side is None else jnp.concatenate([side, taken], axis=1)
        chain = jnp.concatenate([chain, taken], axis=1)
        covered += amount
        hops = covered // length + 1
    other = lax.ppermute(side, "inline", [(0, 1), (1, 0)])
    return side, other, riders


def sum_all(value, axes):
    for axis in axes:
        for distance in bits(lax.axis_size(axis)):
            pairs = swap_pairs(lax.axis_size(axis), distance)
            value = value + lax.ppermute(value, axis, pairs)
    return value


def halving_order(rotation):
    tile = bits(lax.axis_size("tile"))
    rotation = rotation % max(1, len(tile))
    tile = tile[rotation:] + tile[:rotation]
    inline = [("inline", distance) for distance in bits(lax.axis_size("inline"))]
    return inline + [("tile", distance) for distance in tile]


def reduce_shares(kept, given, left, order):
    for step, (axis, distance) in enumerate(order):
        if step or given is None:
            place = left.index((axis, distance))
            bit = (lax.axis_index(axis) // distance) % 2
            given = lax.dynamic_index_in_dim(kept, 1 - bit, place, False).astype(jnp.bfloat16)
            kept = lax.dynamic_index_in_dim(kept, bit, place, False)
            left = left[:place] + left[place + 1 :]
        taken = lax.ppermute(given, axis, swap_pairs(lax.axis_size(axis), distance))
        kept = kept + taken.astype(jnp.float32)
    return kept


class Plan:
    def __init__(self, inline_count, tile_count, inline_cells, depth_cells, chans, shares):
        self.inline_count, self.inline_cells = (inline_count, inline_cells)
        self.depth_cells = depth_cells
        self.inline_total = inline_count * inline_cells
        self.depth_total = tile_count * depth_cells
        self.chans = chans
        self.whole = inline_count == 2 and depth_cells % inline_count == 0
        self.own_depth = depth_cells // inline_count if self.whole else depth_cells
        own = range(self.own_depth)
        spread = lambda cells, d: sorted({z + d * b for z in cells for b in (-1, 0, 1)})
        self.z = {"own": list(own)}
        self.z["second"] = spread(self.z["own"], D2)
        self.z["first"] = spread(self.z["second"], D2)
        self.depth_width = depth_cells + 2 * REACH
        self.z["near1"] = spread(self.z["own"], D1)
        self.z["near2"] = self.z["second"]
        self.z["middle"] = self.z["own"]
        reach = {"own": 0, "second": D2, "first": 2 * D2, "input": REACH, "near1": D1, "near2": D2}
        reach["middle"] = D2
        self.x = {}
        for name, halo in reach.items():
            if self.whole:
                self.x[name] = (0, self.inline_total)
            else:
                self.x[name] = (-halo, inline_cells + halo)
        self.aligned = chans % shares == 0 and inline_count % 2 == 0
        self.groups = shares if self.aligned else chans
        self.per_group = chans // self.groups
        self.pitch = 28 if self.aligned else 32

    def planes(self, name):
        low, high = self.x[name]
        return (high - low) * (self.depth_width if name == "input" else len(self.z[name]))

    def index(self, name, x, z):
        if name == "input":
            start = lax.axis_index("inline") * self.own_depth if self.whole else 0
            return (x - self.x[name][0]) * self.depth_width + z + start + REACH
        return (x - self.x[name][0]) * len(self.z[name]) + self.z[name].index(z)

    def runs(self, name, step):
        low, high = self.x[name]
        found = []
        for x in range(low, high):
            if self.whole:
                taps = tuple(a for a in (-1, 0, 1) if 0 <= x + step * a < self.inline_total)
            else:
                taps = (-1, 0, 1)
            if found and found[-1][0] == taps:
                found[-1][2] += 1
            else:
                found.append([taps, x, 1])
        return found


def depth_base(plan):
    start = lax.axis_index("tile") * plan.depth_cells
    if plan.whole:
        start = start + lax.axis_index("inline") * plan.own_depth
    return start


def inside(plan, x, z):
    depth = depth_base(plan) + z
    good = (depth >= 0) & (depth < plan.depth_total)
    if not plan.whole:
        cell = lax.axis_index("inline") * plan.inline_cells + x
        good = good & (cell >= 0) & (cell < plan.inline_total)
    return good


def each(count, body, unrolled=4):
    if count <= unrolled:
        for i in range(count):
            body(i)
    else:
        lax.fori_loop(0, count, lambda i, carry: (body(i), carry)[1], 0)


def shifted(plane, amount):
    if amount == 0:
        return plane
    width = plane.shape[1]
    column = lax.broadcasted_iota(jnp.int32, plane.shape, 1) + amount
    rolled = pltpu.roll(plane, (-amount) % width, 1)
    return jnp.where((column >= 0) & (column < width), rolled, 0.0)


def store_taps(ref, index, plane, offsets):
    chans = plane.shape[0]
    for place, amount in enumerate(offsets):
        ref[index, place * chans : (place + 1) * chans, :] = shifted(plane, amount).astype(
            jnp.bfloat16
        )


def sigmoid(value):
    return 1.0 / (1.0 + jnp.exp(-value))


def slope_of(value, sig):
    return sig * (1.0 + value * (1.0 - sig))


def matmul(left, right):
    return lax.dot_general(
        left, right, (((1,), (0,)), ((), ())), preferred_element_type=jnp.float32
    )


def matmul_nt(left, right):
    return lax.dot_general(
        left, right, (((1,), (1,)), ((), ())), preferred_element_type=jnp.float32
    )


def conv(weight_ref, taps, columns):
    total = None
    for a in taps:
        term = matmul(weight_ref[a + 1], columns(a))
        total = term if total is None else total + term
    return total


def joined(pieces, axis):
    return pieces[0] if len(pieces) == 1 else jnp.concatenate(pieces, axis=axis)


def softmax_cot(raw, expo, slope, label, scale):
    count = len(raw)
    total = expo[0]
    for n in range(1, count):
        total = total + expo[n]
    found = []
    for n in range(count):
        hit = jnp.where(label == float(n), 1.0, 0.0)
        found.append((expo[n] / total - hit) * slope[n] * scale)
    return found


def load_planes(plan, planes_refs, input_ref, marks_ref):
    chans = plan.chans

    def load(ref, i, to):
        plane = ref[i, :chans, :].astype(jnp.float32)
        store_taps(input_ref, to, plane, (-D1, 0, D1))
        marks_ref[to] = ref[i, chans : chans + LABEL_ROWS, :].astype(jnp.float32)

    if not plan.whole:
        (ref,) = planes_refs
        each(plan.planes("input"), lambda i: load(ref, i, i))
        return
    here = lax.axis_index("inline")
    width = plan.depth_width
    lower = lambda k: REACH - 1 - k
    upper = lambda k: REACH + plan.depth_cells + k
    for ref, fetcher, cells, place in (
        (planes_refs[0], here, plan.depth_cells, lambda k: REACH + k),
        (planes_refs[1], here, REACH, lambda k: jnp.where(here == 0, lower(k), upper(k))),
        (planes_refs[2], 1 - here, REACH, lambda k: jnp.where(here == 0, upper(k), lower(k))),
    ):

        def row(i, ref=ref, fetcher=fetcher, cells=cells, place=place):
            x = lax.rem(i + fetcher * plan.inline_cells, plan.inline_total)
            for k in range(cells):
                load(ref, i * cells + k, x * width + place(k))

        each(plan.inline_total, row, 1)


def forward_kernel(plan, classes, scale, *refs):
    count = 3 if plan.whole else 1
    planes_refs, refs = (refs[:count], refs[count:])
    (
        w1_ref,
        w2_ref,
        rows_ref,
        cols_ref,
        near1_ref,
        near2_ref,
        slope1_ref,
        slope2_ref,
        delta_ref,
        cot_ref,
        stats_ref,
        sums_ref,
        input_ref,
        first_ref,
        base_ref,
        marks_ref,
    ) = refs
    chans = plan.chans
    faults, horizons, salts = classes
    zs = plan.z
    load_planes(plan, planes_refs, input_ref, marks_ref)

    for taps, begin, count in plan.runs("first", D1):

        def first(i, taps=taps, begin=begin):
            x = begin + i

            def columns(a):
                return joined(
                    [
                        joined(
                            [
                                input_ref[plan.index("input", x + D1 * a, z + D1 * b)]
                                for b in (-1, 0, 1)
                            ],
                            0,
                        )
                        for z in zs["first"]
                    ],
                    1,
                )

            pre = conv(w1_ref, taps, columns)
            for j, z in enumerate(zs["first"]):
                value = pre[:, j * 128 : (j + 1) * 128]
                field = input_ref[plan.index("input", x, z), chans : 2 * chans, :]
                sig = sigmoid(value)
                out = field.astype(jnp.float32) + value * sig
                out = out.astype(jnp.bfloat16).astype(jnp.float32)
                out = jnp.where(inside(plan, x, z), out, 0.0)
                store_taps(first_ref, plan.index("first", x, z), out, (-D2, 0, D2))
                if z in zs["own"]:
                    base_ref[plan.index("first", x, z)] = slope_of(value, sig)

        each(count, first)

    own_low, own_high = plan.x["own"]

    def keep_slope(i):
        x = own_low + i
        for z in zs["own"]:
            slope1_ref[plan.index("own", x, z)] = base_ref[plan.index("first", x, z)]

    each(own_high - own_low, keep_slope)

    for name, ref, source, source_ref in (
        ("near1", near1_ref, "input", input_ref),
        ("near2", near2_ref, "first", first_ref),
    ):
        near_low, near_high = plan.x[name]

        def keep(i, name=name, ref=ref, source=source, source_ref=source_ref, near_low=near_low):
            x = near_low + i
            for z in zs[name]:
                ref[plan.index(name, x, z)] = source_ref[plan.index(source, x, z)]

        each(near_high - near_low, keep)

    spread = [
        jnp.broadcast_to(cols_ref[:, n : n + 1], (chans, 128)) for n in range(faults + horizons)
    ]
    for n in range(faults + horizons):
        base_ref[n] = spread[n]

    for taps, begin, count in plan.runs("second", D2):

        def second(i, taps=taps, begin=begin):
            x = begin + i

            def columns(a):
                return joined(
                    [
                        joined(
                            [
                                first_ref[plan.index("first", x + D2 * a, z + D2 * b)]
                                for b in (-1, 0, 1)
                            ],
                            0,
                        )
                        for z in zs["second"]
                    ],
                    1,
                )

            pre = conv(w2_ref, taps, columns)
            field = joined(
                [
                    first_ref[plan.index("first", x, z), chans : 2 * chans, :]
                    for z in zs["second"]
                ],
                1,
            )
            sig = sigmoid(pre)
            slope2 = slope_of(pre, sig)
            second_out = (field.astype(jnp.float32) + pre * sig).astype(jnp.bfloat16)
            raw = matmul(rows_ref[...], second_out)
            squash = jnp.tanh(raw / CAPPING)
            expo = jnp.exp(CAPPING * squash)
            slope = 1.0 - squash * squash
            sums = None
            for j, z in enumerate(zs["second"]):
                lanes = slice(j * 128, (j + 1) * 128)
                row = lambda table, n: table[n : n + 1, lanes]
                marks = marks_ref[plan.index("input", x, z)]
                good = inside(plan, x, z)
                here = plan.index("second", x, z)
                slope2_ref[here] = slope2[:, lanes]
                for task, start, size in ((0, 0, faults), (1, faults, horizons)):
                    span = range(start, start + size)
                    dlog = softmax_cot(
                        [row(raw, n) for n in span],
                        [row(expo, n) for n in span],
                        [row(slope, n) for n in span],
                        marks[task : task + 1, :],
                        scale,
                    )
                    cot = None
                    for n, factor in zip(span, dlog):
                        term = base_ref[n] * factor
                        cot = term if cot is None else cot + term
                    if z in zs["own"]:
                        cot_ref[task, plan.index("middle", x, z)] = cot
                    delta = jnp.where(good, cot * slope2[:, lanes], 0.0)
                    delta_ref[task, here] = delta.astype(jnp.bfloat16)
                query = faults + horizons
                pieces = [row(expo, query)]
                pieces += [row(raw, query + 1 + n) for n in range(salts)]
                pieces += [row(slope, query), marks[2:3, :]]
                for n, piece in enumerate(pieces):
                    stats_ref[here, n : n + 1, :] = piece
                if z in zs["own"]:
                    terms = [pieces[0]] + [pieces[0] * piece for piece in pieces[1 : 1 + salts]]
                    if sums is None:
                        sums = terms
                    else:
                        sums = [old + new for old, new in zip(sums, terms)]
            place = x - plan.x["second"][0]
            sums_ref[place] = jnp.concatenate(
                sums + [jnp.zeros((sums_ref.shape[1] - len(sums), 128), jnp.float32)], 0
            )

        each(count, second)


def salt_cotangents(plan, classes, scale, stats_ref, sums_ref, cols_ref, slope2_ref, delta_ref, cot_ref, spread_ref):
    faults, horizons, salts = classes
    chans = plan.chans
    query = faults + horizons
    for n in range(salts + 1):
        spread_ref[n] = jnp.broadcast_to(cols_ref[:, query + n : query + n + 1], (chans, 128))
    low, high = plan.x["second"]

    def one(i):
        x = low + i
        total = sums_ref[i, 0:1, :]
        salt_raw = [sums_ref[i, 1 + n : 2 + n, :] / total for n in range(salts)]
        squash = [jnp.tanh(value / CAPPING) for value in salt_raw]
        label = stats_ref[plan.index("second", x, 0), salts + 2 : salts + 3, :]
        dlog = softmax_cot(
            salt_raw,
            [jnp.exp(CAPPING * value) for value in squash],
            [1.0 - value * value for value in squash],
            label,
            scale,
        )
        inner = dlog[0] * salt_raw[0]
        for n in range(1, salts):
            inner = inner + dlog[n] * salt_raw[n]
        for z in plan.z["second"]:
            here = plan.index("second", x, z)
            attn = stats_ref[here, 0:1, :] / total
            along = dlog[0] * stats_ref[here, 1:2, :]
            for n in range(1, salts):
                along = along + dlog[n] * stats_ref[here, 1 + n : 2 + n, :]
            dscore = attn * (along - inner) * stats_ref[here, salts + 1 : salts + 2, :]
            cot = spread_ref[0] * dscore
            for n in range(salts):
                cot = cot + spread_ref[1 + n] * (attn * dlog[n])
            cot_ref[0, here] = cot
            delta = jnp.where(inside(plan, x, z), cot * slope2_ref[here], 0.0)
            delta_ref[0, here] = delta.astype(jnp.bfloat16)

    each(high - low, one)


def backward_body(
    plan,
    tasks,
    delta_ref,
    cot_of,
    slope1_ref,
    near1_ref,
    near2_ref,
    w2t_ref,
    outs,
    taps_ref,
    first_delta_ref,
    second_delta_ref,
    rows_refs,
    slots,
):
    chans, zs = (plan.chans, plan.z)
    width = tasks * chans

    def spread(i):
        for task in range(tasks):
            plane = delta_ref[task, i].astype(jnp.float32)
            store_taps(taps_ref, task * plan.planes("second") + i, plane, (D2, 0, -D2))

    each(plan.planes("second"), spread)

    for taps, begin, count in plan.runs("own", -D2):

        def back(i, taps=taps, begin=begin):
            x = begin + i

            def columns(a):
                return joined(
                    [
                        joined(
                            [
                                taps_ref[
                                    task * plan.planes("second")
                                    + plan.index("second", x - D2 * a, z - D2 * b)
                                ]
                                for b in (-1, 0, 1)
                            ],
                            0,
                        )
                        for task in range(tasks)
                        for z in zs["own"]
                    ],
                    1,
                )

            pulled = conv(w2t_ref, taps, columns)
            column = 0
            for task in range(tasks):
                for z in zs["own"]:
                    here = plan.index("own", x, z)
                    cot = cot_of(task, x, z) + pulled[:, column * 128 : (column + 1) * 128]
                    place = slice(task * chans, (task + 1) * chans)
                    first_delta_ref[here, place, :] = (cot * slope1_ref[here]).astype(jnp.bfloat16)
                    second_delta_ref[here, place, :] = delta_ref[task, plan.index("second", x, z)]
                    column += 1

        each(count, back)

    own_low, own_high = plan.x["own"]
    lanes = 128
    for tap in range(27, plan.pitch):
        for ref in rows_refs:
            ref[pl.ds(tap, chans, stride=plan.pitch), :] = jnp.zeros((chans, lanes), jnp.float32)
    for a in (-1, 0, 1):
        for b in (-1, 0, 1):
            chunks = {}
            for ref, name, d, delta_own, begin in (
                (near1_ref, "near1", D1, first_delta_ref, 0),
                (near2_ref, "near2", D2, second_delta_ref, width),
            ):
                cells = []
                for x in range(own_low, own_high):
                    if plan.whole and not 0 <= x + d * a < plan.inline_total:
                        continue
                    cells += [(x, z) for z in zs["own"]]
                left = joined([ref[plan.index(name, x + d * a, z + d * b)] for x, z in cells], 1)
                right = joined([delta_own[plan.index("own", x, z)] for x, z in cells], 1)
                before = begin % lanes
                after = -(before + width) % lanes
                parts = [right]
                if before:
                    parts = [jnp.zeros((before, right.shape[1]), right.dtype)] + parts
                if after:
                    parts = parts + [jnp.zeros((after, right.shape[1]), right.dtype)]
                grad = matmul_nt(left, joined(parts, 0))
                for n in range(grad.shape[1] // lanes):
                    chunk = begin // lanes + n
                    piece = grad[:, n * lanes : (n + 1) * lanes]
                    chunks[chunk] = chunks[chunk] + piece if chunk in chunks else piece
            for chunk, value in chunks.items():
                for c in range(3):
                    tap = 9 * (a + 1) + 3 * (b + 1) + c
                    rows_refs[chunk][pl.ds(tap, chans, stride=plan.pitch), :] = value[
                        c * chans : (c + 1) * chans, :
                    ]
    if plan.aligned:
        kept_ref, given_ref = outs
        half = lax.rem(lax.axis_index("inline"), 2)
        tiles = plan.groups // plan.inline_count
        length = plan.per_group * plan.pitch
        for high in range(plan.inline_count // 2):
            for chunk, ref in enumerate(rows_refs):
                span = slice(chunk * lanes, (chunk + 1) * lanes)
                for target_ref, bit in ((kept_ref, half), (given_ref, 1 - half)):
                    start = pl.multiple_of((2 * high + bit) * tiles * length, 8)
                    block = ref.at[pl.ds(start, tiles * length), :]
                    for j in range(tiles):
                        value = block[j * length : (j + 1) * length, :]
                        target_ref[slots[high * tiles + j], :, span] = value.astype(
                            target_ref.dtype
                        )
    else:
        (out_ref,) = outs

        def write(j):
            for chunk, ref in enumerate(rows_refs):
                start = pl.multiple_of(j * plan.pitch, 8)
                span = slice(chunk * lanes, (chunk + 1) * lanes)
                out_ref[j, :, span] = ref[pl.ds(start, plan.pitch), :]

        each(plan.groups, write)


def pair_kernel(
    plan, slots, delta_ref, cot_ref, slope1_ref, near1_ref, near2_ref, w2t_ref, *rest
):
    outs, scratch = split_refs(plan, rest)
    cot_of = lambda task, x, z: cot_ref[task, plan.index("middle", x, z)]
    backward_body(
        plan,
        2,
        delta_ref,
        cot_of,
        slope1_ref,
        near1_ref,
        near2_ref,
        w2t_ref,
        outs,
        *scratch[:3],
        scratch[3:],
        slots,
    )


def salt_kernel(
    plan,
    slots,
    classes,
    scale,
    stats_ref,
    sums_ref,
    cols_ref,
    slope2_ref,
    slope1_ref,
    near1_ref,
    near2_ref,
    w2t_ref,
    *rest,
):
    outs, scratch = split_refs(plan, rest)
    delta_ref, cot_ref, spread_ref = scratch[:3]
    salt_cotangents(
        plan,
        classes,
        scale,
        stats_ref,
        sums_ref,
        cols_ref,
        slope2_ref,
        delta_ref,
        cot_ref,
        spread_ref,
    )
    cot_of = lambda task, x, z: cot_ref[task, plan.index("second", x, z)]
    backward_body(
        plan,
        1,
        delta_ref,
        cot_of,
        slope1_ref,
        near1_ref,
        near2_ref,
        w2t_ref,
        outs,
        *scratch[3:6],
        scratch[6:],
        slots,
    )


def split_refs(plan, refs):
    count = 2 if plan.aligned else 1
    return (refs[:count], refs[count:])


def vmem(count):
    return [pl.BlockSpec(memory_space=pltpu.VMEM)] * count


def backward_shapes(plan, tasks):
    chans = plan.chans
    width = round_up(2 * tasks * chans, 128)
    if plan.aligned:
        shape = (plan.groups // 2, plan.per_group * plan.pitch, width)
        outs = [jax.ShapeDtypeStruct(shape, jnp.float32), jax.ShapeDtypeStruct(shape, jnp.bfloat16)]
    else:
        outs = [jax.ShapeDtypeStruct((plan.groups, plan.pitch, width), jnp.float32)]
    scratch = [
        pltpu.VMEM((tasks * plan.planes("second"), 3 * chans, 128), jnp.bfloat16),
        pltpu.VMEM((plan.planes("own"), tasks * chans, 128), jnp.bfloat16),
        pltpu.VMEM((plan.planes("own"), tasks * chans, 128), jnp.bfloat16),
    ]
    scratch += [pltpu.VMEM((chans * plan.pitch, 128), jnp.float32)] * (width // 128)
    return (outs, scratch)


def tap_major(weight, flip):
    ins, _, outs = weight.shape
    parts = weight.reshape(ins, 3, 9, outs)
    if flip:
        return parts.transpose(1, 0, 2, 3).reshape(3, ins, 9 * outs)
    return parts.transpose(1, 3, 2, 0).reshape(3, outs, 9 * ins)


def slots_of(plan, order):
    if not plan.aligned:
        return None
    tiles = plan.groups // plan.inline_count
    slots = []
    for high in range(plan.inline_count // 2):
        for tile in range(tiles):
            slot = 0
            for axis, distance in order[1:]:
                index = 2 * high if axis == "inline" else tile
                slot = 2 * slot + index // distance % 2
            slots.append(slot)
    return slots


def on_device(
    features,
    conv1_weight,
    conv2_weight,
    fault_head,
    horizon_head,
    salt_query,
    salt_head,
    fault_labels,
    horizon_labels,
    salt_labels,
):
    chans, inline_cells, depth_cells, cross_cells = features.shape
    inline_count, tile_count = (lax.axis_size("inline"), lax.axis_size("tile"))
    shares = inline_count * tile_count
    plan = Plan(inline_count, tile_count, inline_cells, depth_cells, chans, shares)
    scale = 1.0 / math.sqrt(plan.inline_total * plan.depth_total * cross_cells)
    classes = (fault_head.shape[1], horizon_head.shape[1], salt_head.shape[1])

    marks = jnp.stack(
        [
            fault_labels,
            horizon_labels,
            jnp.broadcast_to(salt_labels[:, None, :], fault_labels.shape),
        ],
        axis=2,
    ).astype(jnp.bfloat16)
    marks = jnp.pad(marks, ((0, 0), (0, 0), (0, LABEL_ROWS - 3), (0, 0)))
    planes = jnp.concatenate([features.transpose(1, 2, 0, 3), marks], axis=2)
    cols = jnp.concatenate([fault_head, horizon_head, salt_query[:, None], salt_head], axis=1)
    cols = jnp.pad(cols, ((0, 0), (0, 16 - cols.shape[1])))
    riders = [
        cols.T,
        cols.astype(jnp.float32),
        tap_major(conv1_weight, False),
        tap_major(conv2_weight, False),
        tap_major(conv2_weight, True),
    ]
    if plan.whole:
        other = lax.ppermute(planes, "inline", [(0, 1), (1, 0)])
        planes = jnp.concatenate([planes, other], axis=0)
        mine, theirs, riders = outward(planes, REACH, riders)
        sources = [planes, mine, theirs]
    else:
        planes = window(planes, "tile", 1, REACH)
        sources = [window(planes, "inline", 0, REACH)]
    sources = [source.reshape((-1,) + source.shape[2:]) for source in sources]
    rows, cols, w1, w2, w2t = riders

    f32, bf16 = (jnp.float32, jnp.bfloat16)
    own, second = (plan.planes("own"), plan.planes("second"))
    second_x = plan.x["second"][1] - plan.x["second"][0]
    shape = jax.ShapeDtypeStruct
    near1, near2, slope1, slope2, delta, cot, stats, sums = pl.pallas_call(
        functools.partial(forward_kernel, plan, classes, scale),
        out_shape=[
            shape((plan.planes("near1"), 3 * chans, 128), bf16),
            shape((plan.planes("near2"), 3 * chans, 128), bf16),
            shape((own, chans, 128), f32),
            shape((second, chans, 128), f32),
            shape((2, second, chans, 128), bf16),
            shape((2, plan.planes("middle"), chans, 128), f32),
            shape((second, 8, 128), f32),
            shape((second_x, 8, 128), f32),
        ],
        in_specs=vmem(len(sources) + 4),
        out_specs=vmem(8),
        scratch_shapes=[
            pltpu.VMEM((plan.planes("input"), 3 * chans, 128), bf16),
            pltpu.VMEM((plan.planes("first"), 3 * chans, 128), bf16),
            pltpu.VMEM((plan.planes("first"), chans, 128), f32),
            pltpu.VMEM((plan.planes("input"), LABEL_ROWS, 128), f32),
        ],
        name="forward",
    )(*sources, w1, w2, rows, cols)

    sums = sum_all(sums, AXES if plan.whole else ("tile",))

    orders = [halving_order(0), halving_order(1)]
    outs, scratch = backward_shapes(plan, 2)
    pair = pl.pallas_call(
        functools.partial(pair_kernel, plan, slots_of(plan, orders[0])),
        out_shape=outs,
        in_specs=vmem(6),
        out_specs=vmem(len(outs)),
        scratch_shapes=scratch,
        name="pair",
    )(delta, cot, slope1, near1, near2, w2t)
    sums, *pair = lax.optimization_barrier((sums, *pair))
    outs, scratch = backward_shapes(plan, 1)
    scratch = [
        pltpu.VMEM((1, second, chans, 128), bf16),
        pltpu.VMEM((1, second, chans, 128), f32),
        pltpu.VMEM((1 + classes[2], chans, 128), f32),
    ] + scratch
    salt = pl.pallas_call(
        functools.partial(
            salt_kernel, plan, slots_of(plan, orders[1]), classes, plan.depth_total * scale
        ),
        out_shape=outs,
        in_specs=vmem(8),
        out_specs=vmem(len(outs)),
        scratch_shapes=scratch,
        name="salt",
    )(stats, sums, cols, slope2, slope1, near1, near2, w2t)

    terms = []
    if plan.aligned:
        for (kept, given), tasks, order in ((pair, 2, orders[0]), (salt, 1, orders[1])):
            kept = kept.reshape((2,) * (len(order) - 1) + kept.shape[1:])
            given = given.reshape(kept.shape)
            share = reduce_shares(kept, given, order[1:], order)
            share = share.reshape(plan.per_group, plan.pitch, -1)
            share = share[:, :27, : 2 * tasks * chans].reshape(-1, 2, tasks, chans)
            terms.append(share.transpose(1, 2, 0, 3).reshape(2, tasks, -1))
        grads = jnp.concatenate(terms, axis=1)
    else:
        for (value,), tasks in ((pair, 2), (salt, 1)):
            value = value[:, :27, : 2 * tasks * chans].reshape(chans, 27, 2, tasks, chans)
            terms.append(value.transpose(2, 3, 0, 1, 4).reshape(2, tasks, shares, -1))
        flat = jnp.concatenate(terms, axis=1).transpose(2, 0, 1, 3)
        left = [(axis, d) for axis in AXES for d in reversed(bits(lax.axis_size(axis)))]
        flat = flat.reshape((2,) * len(left) + flat.shape[1:])
        grads = reduce_shares(flat, None, left, orders[0])
    gram = jnp.sum(grads[:, :, None, :] * grads[:, None, :, :], axis=3)
    gram = sum_all(gram, AXES) / (27 * chans * chans)
    return (grads, gram)


def solution(mesh):
    in_specs = (
        P(None, "inline", "tile", None),
        P(),
        P(),
        P(),
        P(),
        P(),
        P(),
        P("inline", "tile", None),
        P("inline", "tile", None),
        P("inline", None),
    )
    out_specs = (P(None, None, ("inline", "tile")), P())
    return jax.shard_map(
        on_device, mesh=mesh, in_specs=in_specs, out_specs=out_specs, check_vma=False
    )
```

```python
import functools
import math

import jax
import jax.numpy as jnp
from jax import lax
from jax.experimental import pallas as pl
from jax.experimental.pallas import tpu as pltpu
from jax.experimental.layout import Layout, with_layout_constraint
from jax.sharding import PartitionSpec as P


D1 = 1
D2 = 2
REACH = D1 + 2 * D2

CAPPING = 8.0
LABEL_ROWS = 8
AXES = ("inline", "tile")


def round_up(value, unit):
    return -(-value // unit) * unit


def bits(count):
    return [1 << bit for bit in range(count.bit_length() - 1)]


def swap_pairs(count, distance):
    return [(i, i ^ distance) for i in range(count)]


def window(cells, axis, dim, halo):
    count, length = (lax.axis_size(axis), cells.shape[dim])
    covered, hops = (0, 1)
    while covered < halo:
        amount = min(halo - covered, length + covered)
        size = cells.shape[dim]
        start = lax.slice_in_dim(cells, covered, covered + amount, axis=dim)
        end = lax.slice_in_dim(cells, size - covered - amount, size - covered, axis=dim)
        up = [(i, i + hops) for i in range(count - hops)]
        down = [(j, i) for i, j in up]
        before = lax.ppermute(end, axis, up)
        after = lax.ppermute(start, axis, down)
        cells = jnp.concatenate([before, cells, after], axis=dim)
        covered += amount
        hops = covered // length + 1
    return cells


def outward(cells, halo, needed, riders):
    ready = []
    here, length = (lax.axis_index("inline"), cells.shape[1])
    count = lax.axis_size("tile")
    chain = jnp.where(here == 0, cells[:, ::-1], cells)
    side = None
    covered, hops = (0, 1)
    while covered < halo:
        amount = min(halo - covered, length + covered)
        pairs = [(i, i + hops) for i in range(count - hops)]
        pairs += [(count + j, count + i) for i, j in pairs]
        taken = lax.ppermute(chain[:, :amount], AXES, pairs)
        if riders:
            taken, *made = lax.optimization_barrier((taken, *riders.pop(0)))
            ready += made
        side = taken if side is None else jnp.concatenate([side, taken], axis=1)
        chain = jnp.concatenate([chain, taken], axis=1)
        covered += amount
        hops = covered // length + 1
    for group in riders:
        ready += group
    other = lax.ppermute(side[:, :needed], "inline", [(0, 1), (1, 0)])
    return side, other, ready


def share_sums(value, axes):
    copies = jnp.broadcast_to(value, (lax.axis_size(axes),) + value.shape)
    return jnp.sum(lax.all_to_all(copies, axes, 0, 0), axis=0)


def halving_order(first):
    tile = bits(lax.axis_size("tile"))
    tile = tile[first : first + 1] + tile[:first] + tile[first + 1 :]
    inline = [("inline", distance) for distance in bits(lax.axis_size("inline"))]
    return inline + [("tile", distance) for distance in tile]


def halve(kept, axis, distance):
    half = kept.shape[0] // 2
    bit = (lax.axis_index(axis) // distance) % 2
    given = lax.dynamic_slice_in_dim(kept, (1 - bit) * half, half, 0).astype(jnp.bfloat16)
    return lax.dynamic_slice_in_dim(kept, bit * half, half, 0), given


def exchange(kept, given, axis, distance, after=None):
    taken = lax.ppermute(given, axis, swap_pairs(lax.axis_size(axis), distance))
    if after is not None:
        taken, _ = lax.optimization_barrier((taken, after))
    return kept + taken.astype(jnp.float32)


def first_halving(kept, given, order):
    kept = exchange(kept, given, *order[0])
    return halve(kept, *order[1])


def reduce_shares(chains, orders):
    chains = list(chains)
    for step in range(len(orders[0])):
        for n, order in enumerate(orders):
            after = chains[n - 1][1] if len(chains) > 1 else None
            kept = exchange(*chains[n], *order[step], after)
            last = step + 1 == len(order)
            chains[n] = (kept, None) if last else halve(kept, *order[step + 1])
    return [kept for kept, _ in chains]


class Plan:
    def __init__(self, inline_count, tile_count, inline_cells, depth_cells, chans, shares):
        self.inline_count, self.inline_cells = (inline_count, inline_cells)
        self.depth_cells = depth_cells
        self.inline_total = inline_count * inline_cells
        self.depth_total = tile_count * depth_cells
        self.chans = chans
        self.whole = inline_count == 2 and depth_cells % inline_count == 0
        self.own_depth = depth_cells // inline_count if self.whole else depth_cells
        own = range(self.own_depth)
        spread = lambda cells, d: sorted({z + d * b for z in cells for b in (-1, 0, 1)})
        self.z = {"own": list(own)}
        self.z["second"] = spread(self.z["own"], D2)
        self.z["first"] = spread(self.z["second"], D2)
        self.depth_width = depth_cells + 2 * REACH
        self.partner_reach = REACH
        self.z["near1"] = spread(self.z["own"], D1)
        self.z["near2"] = self.z["second"]
        self.z["middle"] = self.z["own"]
        reach = {"own": 0, "second": D2, "first": 2 * D2, "input": REACH, "near1": D1, "near2": D2}
        reach["middle"] = D2
        self.x = {}
        for name, halo in reach.items():
            if self.whole:
                self.x[name] = (0, self.inline_total)
            else:
                self.x[name] = (-halo, inline_cells + halo)
        self.aligned = chans % shares == 0 and inline_count % 2 == 0
        self.groups = shares if self.aligned else chans
        self.per_group = chans // self.groups
        self.pitch = 28 if self.aligned else 32
        self.rows = round_up(self.per_group * self.pitch, 8)

    def planes(self, name):
        low, high = self.x[name]
        return (high - low) * (self.depth_width if name == "input" else len(self.z[name]))

    def index(self, name, x, z):
        if name == "input":
            start = lax.axis_index("inline") * self.own_depth if self.whole else 0
            return (x - self.x[name][0]) * self.depth_width + z + start + REACH
        return (x - self.x[name][0]) * len(self.z[name]) + self.z[name].index(z)

    def runs(self, name, step):
        low, high = self.x[name]
        found = []
        for x in range(low, high):
            if self.whole:
                taps = tuple(a for a in (-1, 0, 1) if 0 <= x + step * a < self.inline_total)
            else:
                taps = (-1, 0, 1)
            if found and found[-1][0] == taps:
                found[-1][2] += 1
            else:
                found.append([taps, x, 1])
        return found


def depth_base(plan):
    start = lax.axis_index("tile") * plan.depth_cells
    if plan.whole:
        start = start + lax.axis_index("inline") * plan.own_depth
    return start


def inside(plan, x, z):
    depth = depth_base(plan) + z
    good = (depth >= 0) & (depth < plan.depth_total)
    if not plan.whole:
        cell = lax.axis_index("inline") * plan.inline_cells + x
        good = good & (cell >= 0) & (cell < plan.inline_total)
    return good


def each(count, body, unrolled=4):
    if count <= unrolled:
        for i in range(count):
            body(i)
    else:
        lax.fori_loop(0, count, lambda i, carry: (body(i), carry)[1], 0)


def shifted(plane, amount):
    if amount == 0:
        return plane
    width = plane.shape[1]
    column = lax.broadcasted_iota(jnp.int32, plane.shape, 1) + amount
    rolled = pltpu.roll(plane, (-amount) % width, 1)
    return jnp.where((column >= 0) & (column < width), rolled, 0.0)


def store_taps(ref, index, plane, offsets):
    chans = plane.shape[0]
    for place, amount in enumerate(offsets):
        ref[index, place * chans : (place + 1) * chans, :] = shifted(plane, amount).astype(
            jnp.bfloat16
        )


def sigmoid(value):
    return 1.0 / (1.0 + jnp.exp(-value))


def slope_of(value, sig):
    return sig * (1.0 + value * (1.0 - sig))


def matmul(left, right):
    return lax.dot_general(
        left, right, (((1,), (0,)), ((), ())), preferred_element_type=jnp.float32
    )


def matmul_nt(left, right):
    return lax.dot_general(
        left, right, (((1,), (1,)), ((), ())), preferred_element_type=jnp.float32
    )


def conv(weight_ref, taps, columns):
    total = None
    for a in taps:
        term = matmul(weight_ref[a + 1], columns(a))
        total = term if total is None else total + term
    return total


def joined(pieces, axis):
    return pieces[0] if len(pieces) == 1 else jnp.concatenate(pieces, axis=axis)


def softmax_cot(raw, expo, slope, label, scale):
    count = len(raw)
    total = expo[0]
    for n in range(1, count):
        total = total + expo[n]
    found = []
    for n in range(count):
        hit = jnp.where(label == float(n), 1.0, 0.0)
        found.append((expo[n] / total - hit) * slope[n] * scale)
    return found


def load_planes(plan, planes_refs, input_ref, marks_ref):
    chans = plan.chans

    def load(ref, i, to):
        plane = ref[i, :chans, :].astype(jnp.float32)
        store_taps(input_ref, to, plane, (-D1, 0, D1))
        marks_ref[to] = ref[i, chans : chans + LABEL_ROWS, :].astype(jnp.float32)

    if not plan.whole:
        (ref,) = planes_refs
        each(plan.planes("input"), lambda i: load(ref, i, i))
        return
    here = lax.axis_index("inline")
    width = plan.depth_width
    lower = lambda k: REACH - 1 - k
    upper = lambda k: REACH + plan.depth_cells + k
    for ref, fetcher, cells, place in (
        (planes_refs[0], here, plan.depth_cells, lambda k: REACH + k),
        (planes_refs[1], here, REACH, lambda k: jnp.where(here == 0, lower(k), upper(k))),
        (planes_refs[2], 1 - here, plan.partner_reach, lambda k: jnp.where(here == 0, upper(k), lower(k))),
    ):

        def row(i, ref=ref, fetcher=fetcher, cells=cells, place=place):
            x = lax.rem(i + fetcher * plan.inline_cells, plan.inline_total)
            for k in range(cells):
                load(ref, i * cells + k, x * width + place(k))

        each(plan.inline_total, row, 1)


def forward_kernel(plan, classes, scale, *refs):
    count = 3 if plan.whole else 1
    planes_refs, refs = (refs[:count], refs[count:])
    (
        w1_ref,
        w2_ref,
        rows_ref,
        cols_ref,
        near1_ref,
        near2_ref,
        slope1_ref,
        slope2_ref,
        delta_ref,
        cot_ref,
        stats_ref,
        sums_ref,
        input_ref,
        first_ref,
        base_ref,
        marks_ref,
    ) = refs
    chans = plan.chans
    faults, horizons, salts = classes
    zs = plan.z
    load_planes(plan, planes_refs, input_ref, marks_ref)

    for taps, begin, count in plan.runs("first", D1):

        def first(i, taps=taps, begin=begin):
            x = begin + i

            def columns(a):
                return joined(
                    [
                        joined(
                            [
                                input_ref[plan.index("input", x + D1 * a, z + D1 * b)]
                                for b in (-1, 0, 1)
                            ],
                            0,
                        )
                        for z in zs["first"]
                    ],
                    1,
                )

            pre = conv(w1_ref, taps, columns)
            for j, z in enumerate(zs["first"]):
                value = pre[:, j * 128 : (j + 1) * 128]
                field = input_ref[plan.index("input", x, z), chans : 2 * chans, :]
                sig = sigmoid(value)
                out = field.astype(jnp.float32) + value * sig
                out = out.astype(jnp.bfloat16).astype(jnp.float32)
                out = jnp.where(inside(plan, x, z), out, 0.0)
                store_taps(first_ref, plan.index("first", x, z), out, (-D2, 0, D2))
                if z in zs["own"]:
                    base_ref[plan.index("first", x, z)] = slope_of(value, sig)

        each(count, first)

    own_low, own_high = plan.x["own"]

    def keep_slope(i):
        x = own_low + i
        for z in zs["own"]:
            slope1_ref[plan.index("own", x, z)] = base_ref[plan.index("first", x, z)]

    each(own_high - own_low, keep_slope)

    for name, ref, source, source_ref in (
        ("near1", near1_ref, "input", input_ref),
        ("near2", near2_ref, "first", first_ref),
    ):
        near_low, near_high = plan.x[name]

        def keep(i, name=name, ref=ref, source=source, source_ref=source_ref, near_low=near_low):
            x = near_low + i
            for z in zs[name]:
                ref[plan.index(name, x, z)] = source_ref[plan.index(source, x, z)]

        each(near_high - near_low, keep)

    spread = [
        jnp.broadcast_to(cols_ref[:, n : n + 1], (chans, 128)) for n in range(faults + horizons)
    ]
    for n in range(faults + horizons):
        base_ref[n] = spread[n]

    used = (plan.x["second"][1] - plan.x["second"][0]) * (1 + salts)
    if used < sums_ref.shape[0]:
        sums_ref[used:, :] = jnp.zeros((sums_ref.shape[0] - used, 128), jnp.float32)

    for taps, begin, count in plan.runs("second", D2):

        def second(i, taps=taps, begin=begin):
            x = begin + i

            def columns(a):
                return joined(
                    [
                        joined(
                            [
                                first_ref[plan.index("first", x + D2 * a, z + D2 * b)]
                                for b in (-1, 0, 1)
                            ],
                            0,
                        )
                        for z in zs["second"]
                    ],
                    1,
                )

            pre = conv(w2_ref, taps, columns)
            field = joined(
                [
                    first_ref[plan.index("first", x, z), chans : 2 * chans, :]
                    for z in zs["second"]
                ],
                1,
            )
            sig = sigmoid(pre)
            slope2 = slope_of(pre, sig)
            second_out = (field.astype(jnp.float32) + pre * sig).astype(jnp.bfloat16)
            raw = matmul(rows_ref[...], second_out)
            squash = jnp.tanh(raw / CAPPING)
            expo = jnp.exp(CAPPING * squash)
            slope = 1.0 - squash * squash
            sums = None
            for j, z in enumerate(zs["second"]):
                lanes = slice(j * 128, (j + 1) * 128)
                row = lambda table, n: table[n : n + 1, lanes]
                marks = marks_ref[plan.index("input", x, z)]
                good = inside(plan, x, z)
                here = plan.index("second", x, z)
                slope2_ref[here] = slope2[:, lanes]
                for task, start, size in ((0, 0, faults), (1, faults, horizons)):
                    span = range(start, start + size)
                    dlog = softmax_cot(
                        [row(raw, n) for n in span],
                        [row(expo, n) for n in span],
                        [row(slope, n) for n in span],
                        marks[task : task + 1, :],
                        scale,
                    )
                    cot = None
                    for n, factor in zip(span, dlog):
                        term = base_ref[n] * factor
                        cot = term if cot is None else cot + term
                    if z in zs["own"]:
                        cot_ref[task, plan.index("middle", x, z)] = cot
                    delta = jnp.where(good, cot * slope2[:, lanes], 0.0)
                    delta_ref[task, here] = delta.astype(jnp.bfloat16)
                query = faults + horizons
                pieces = [row(expo, query)]
                pieces += [row(raw, query + 1 + n) for n in range(salts)]
                pieces += [row(slope, query), marks[2:3, :]]
                for n, piece in enumerate(pieces):
                    stats_ref[here, n : n + 1, :] = piece
                if z in zs["own"]:
                    terms = [pieces[0]] + [pieces[0] * piece for piece in pieces[1 : 1 + salts]]
                    if sums is None:
                        sums = terms
                    else:
                        sums = [old + new for old, new in zip(sums, terms)]
            place = x - plan.x["second"][0]
            for n, piece in enumerate(sums):
                sums_ref[pl.ds(place * (1 + salts) + n, 1), :] = piece

        each(count, second)


def salt_cotangents(plan, classes, scale, stats_ref, sums_ref, cols_ref, slope2_ref, delta_ref, cot_ref, spread_ref):
    faults, horizons, salts = classes
    chans = plan.chans
    query = faults + horizons
    for n in range(salts + 1):
        spread_ref[n] = jnp.broadcast_to(cols_ref[:, query + n : query + n + 1], (chans, 128))
    low, high = plan.x["second"]

    def one(i):
        x = low + i
        sums = [sums_ref[pl.ds(i * (1 + salts) + n, 1), :] for n in range(1 + salts)]
        total = sums[0]
        salt_raw = [value / total for value in sums[1:]]
        squash = [jnp.tanh(value / CAPPING) for value in salt_raw]
        label = stats_ref[plan.index("second", x, 0), salts + 2 : salts + 3, :]
        dlog = softmax_cot(
            salt_raw,
            [jnp.exp(CAPPING * value) for value in squash],
            [1.0 - value * value for value in squash],
            label,
            scale,
        )
        inner = dlog[0] * salt_raw[0]
        for n in range(1, salts):
            inner = inner + dlog[n] * salt_raw[n]
        for z in plan.z["second"]:
            here = plan.index("second", x, z)
            attn = stats_ref[here, 0:1, :] / total
            along = dlog[0] * stats_ref[here, 1:2, :]
            for n in range(1, salts):
                along = along + dlog[n] * stats_ref[here, 1 + n : 2 + n, :]
            dscore = attn * (along - inner) * stats_ref[here, salts + 1 : salts + 2, :]
            cot = spread_ref[0] * dscore
            for n in range(salts):
                cot = cot + spread_ref[1 + n] * (attn * dlog[n])
            cot_ref[0, here] = cot
            delta = jnp.where(inside(plan, x, z), cot * slope2_ref[here], 0.0)
            delta_ref[0, here] = delta.astype(jnp.bfloat16)

    each(high - low, one)


def backward_body(
    plan,
    tasks,
    delta_ref,
    cot_of,
    slope1_ref,
    near1_ref,
    near2_ref,
    w2t_ref,
    outs,
    taps_ref,
    first_delta_ref,
    second_delta_ref,
    rows_refs,
    slots,
):
    chans, zs = (plan.chans, plan.z)
    width = tasks * chans

    def spread(i):
        for task in range(tasks):
            plane = delta_ref[task, i].astype(jnp.float32)
            store_taps(taps_ref, task * plan.planes("second") + i, plane, (D2, 0, -D2))

    each(plan.planes("second"), spread)

    for taps, begin, count in plan.runs("own", -D2):

        def back(i, taps=taps, begin=begin):
            x = begin + i

            def columns(a):
                return joined(
                    [
                        joined(
                            [
                                taps_ref[
                                    task * plan.planes("second")
                                    + plan.index("second", x - D2 * a, z - D2 * b)
                                ]
                                for b in (-1, 0, 1)
                            ],
                            0,
                        )
                        for task in range(tasks)
                        for z in zs["own"]
                    ],
                    1,
                )

            pulled = conv(w2t_ref, taps, columns)
            column = 0
            for task in range(tasks):
                for z in zs["own"]:
                    here = plan.index("own", x, z)
                    cot = cot_of(task, x, z) + pulled[:, column * 128 : (column + 1) * 128]
                    place = slice(task * chans, (task + 1) * chans)
                    first_delta_ref[here, place, :] = (cot * slope1_ref[here]).astype(jnp.bfloat16)
                    second_delta_ref[here, place, :] = delta_ref[task, plan.index("second", x, z)]
                    column += 1

        each(count, back)

    own_low, own_high = plan.x["own"]
    lanes = 128
    for ref in rows_refs:
        ref[chans * plan.pitch :, :] = jnp.zeros((8, lanes), jnp.float32)
    for tap in range(27, plan.pitch):
        for ref in rows_refs:
            ref[pl.ds(tap, chans, stride=plan.pitch), :] = jnp.zeros((chans, lanes), jnp.float32)
    for a in (-1, 0, 1):
        for b in (-1, 0, 1):
            chunks = {}
            for ref, name, d, delta_own, begin in (
                (near1_ref, "near1", D1, first_delta_ref, 0),
                (near2_ref, "near2", D2, second_delta_ref, width),
            ):
                cells = []
                for x in range(own_low, own_high):
                    if plan.whole and not 0 <= x + d * a < plan.inline_total:
                        continue
                    cells += [(x, z) for z in zs["own"]]
                left = joined([ref[plan.index(name, x + d * a, z + d * b)] for x, z in cells], 1)
                right = joined([delta_own[plan.index("own", x, z)] for x, z in cells], 1)
                before = begin % lanes
                after = -(before + width) % lanes
                parts = [right]
                if before:
                    parts = [jnp.zeros((before, right.shape[1]), right.dtype)] + parts
                if after:
                    parts = parts + [jnp.zeros((after, right.shape[1]), right.dtype)]
                grad = matmul_nt(left, joined(parts, 0))
                for n in range(grad.shape[1] // lanes):
                    chunk = begin // lanes + n
                    piece = grad[:, n * lanes : (n + 1) * lanes]
                    chunks[chunk] = chunks[chunk] + piece if chunk in chunks else piece
            for chunk, value in chunks.items():
                for c in range(3):
                    tap = 9 * (a + 1) + 3 * (b + 1) + c
                    rows_refs[chunk][pl.ds(tap, chans, stride=plan.pitch), :] = value[
                        c * chans : (c + 1) * chans, :
                    ]
    if plan.aligned:
        kept_ref, given_ref = outs
        half = lax.rem(lax.axis_index("inline"), 2)
        tiles = plan.groups // plan.inline_count
        length = plan.per_group * plan.pitch
        for high in range(plan.inline_count // 2):
            for chunk, ref in enumerate(rows_refs):
                span = slice(chunk * lanes, (chunk + 1) * lanes)
                for target_ref, bit in ((kept_ref, half), (given_ref, 1 - half)):
                    start = pl.multiple_of((2 * high + bit) * tiles * length, 8)
                    block = ref.at[pl.ds(start, tiles * length + 8), :]
                    for j in range(tiles):
                        value = block[j * length : j * length + plan.rows, :]
                        target_ref[slots[high * tiles + j], :, span] = value.astype(
                            target_ref.dtype
                        )
    else:
        (out_ref,) = outs

        def write(j):
            for chunk, ref in enumerate(rows_refs):
                start = pl.multiple_of(j * plan.pitch, 8)
                span = slice(chunk * lanes, (chunk + 1) * lanes)
                out_ref[j, :, span] = ref[pl.ds(start, plan.pitch), :]

        each(plan.groups, write)


def pair_kernel(
    plan, slots, delta_ref, cot_ref, slope1_ref, near1_ref, near2_ref, w2t_ref, *rest
):
    outs, scratch = split_refs(plan, rest)
    cot_of = lambda task, x, z: cot_ref[task, plan.index("middle", x, z)]
    backward_body(
        plan,
        2,
        delta_ref,
        cot_of,
        slope1_ref,
        near1_ref,
        near2_ref,
        w2t_ref,
        outs,
        *scratch[:3],
        scratch[3:],
        slots,
    )


def salt_kernel(
    plan,
    slots,
    classes,
    scale,
    stats_ref,
    sums_ref,
    cols_ref,
    slope2_ref,
    slope1_ref,
    near1_ref,
    near2_ref,
    w2t_ref,
    *rest,
):
    outs, scratch = split_refs(plan, rest)
    delta_ref, cot_ref, spread_ref = scratch[:3]
    salt_cotangents(
        plan,
        classes,
        scale,
        stats_ref,
        sums_ref,
        cols_ref,
        slope2_ref,
        delta_ref,
        cot_ref,
        spread_ref,
    )
    cot_of = lambda task, x, z: cot_ref[task, plan.index("second", x, z)]
    backward_body(
        plan,
        1,
        delta_ref,
        cot_of,
        slope1_ref,
        near1_ref,
        near2_ref,
        w2t_ref,
        outs,
        *scratch[3:6],
        scratch[6:],
        slots,
    )


def split_refs(plan, refs):
    count = 2 if plan.aligned else 1
    return (refs[:count], refs[count:])


def vmem(count):
    return [pl.BlockSpec(memory_space=pltpu.VMEM)] * count


def backward_shapes(plan, tasks):
    chans = plan.chans
    width = round_up(2 * tasks * chans, 128)
    if plan.aligned:
        shape = (plan.groups // 2, plan.rows, width)
        outs = [jax.ShapeDtypeStruct(shape, jnp.float32), jax.ShapeDtypeStruct(shape, jnp.bfloat16)]
    else:
        outs = [jax.ShapeDtypeStruct((plan.groups, plan.pitch, width), jnp.float32)]
    scratch = [
        pltpu.VMEM((tasks * plan.planes("second"), 3 * chans, 128), jnp.bfloat16),
        pltpu.VMEM((plan.planes("own"), tasks * chans, 128), jnp.bfloat16),
        pltpu.VMEM((plan.planes("own"), tasks * chans, 128), jnp.bfloat16),
    ]
    scratch += [pltpu.VMEM((chans * plan.pitch + 8, 128), jnp.float32)] * (width // 128)
    return (outs, scratch)


def tap_major(weight, flip):
    ins, _, outs = weight.shape
    parts = weight.reshape(ins, 3, 9, outs)
    if flip:
        parts = parts.transpose(1, 0, 2, 3).reshape(3, ins, 9 * outs)
    else:
        parts = parts.transpose(1, 3, 2, 0).reshape(3, outs, 9 * ins)
    return with_layout_constraint(parts, Layout(major_to_minor=(0, 1, 2)))


def slots_of(plan, order):
    if not plan.aligned:
        return None
    tiles = plan.groups // plan.inline_count
    slots = []
    for high in range(plan.inline_count // 2):
        for tile in range(tiles):
            slot = 0
            for axis, distance in order[1:]:
                index = 2 * high if axis == "inline" else tile
                slot = 2 * slot + index // distance % 2
            slots.append(slot)
    return slots


def on_device(
    features,
    conv1_weight,
    conv2_weight,
    fault_head,
    horizon_head,
    salt_query,
    salt_head,
    fault_labels,
    horizon_labels,
    salt_labels,
):
    chans, inline_cells, depth_cells, cross_cells = features.shape
    inline_count, tile_count = (lax.axis_size("inline"), lax.axis_size("tile"))
    shares = inline_count * tile_count
    plan = Plan(inline_count, tile_count, inline_cells, depth_cells, chans, shares)
    scale = 1.0 / math.sqrt(plan.inline_total * plan.depth_total * cross_cells)
    classes = (fault_head.shape[1], horizon_head.shape[1], salt_head.shape[1])

    marks = jnp.stack(
        [
            fault_labels,
            horizon_labels,
            jnp.broadcast_to(salt_labels[:, None, :], fault_labels.shape),
        ],
        axis=2,
    ).astype(jnp.bfloat16)
    marks = jnp.pad(marks, ((0, 0), (0, 0), (0, LABEL_ROWS - 3), (0, 0)))
    planes = jnp.concatenate([features.transpose(1, 2, 0, 3), marks], axis=2)
    cols = jnp.concatenate([fault_head, horizon_head, salt_query[:, None], salt_head], axis=1)
    cols = jnp.pad(cols, ((0, 0), (0, 16 - cols.shape[1])))
    riders = [
        [cols.T, cols.astype(jnp.float32), tap_major(conv1_weight, False)],
        [tap_major(conv2_weight, False), tap_major(conv2_weight, True)],
    ]
    if plan.whole:
        other = lax.ppermute(planes, "inline", [(0, 1), (1, 0)])
        planes = jnp.concatenate([planes, other], axis=0)
        mine, theirs, riders = outward(planes, REACH, plan.partner_reach, riders)
        sources = [planes, mine, theirs]
    else:
        planes = window(planes, "tile", 1, REACH)
        sources = [window(planes, "inline", 0, REACH)]
        riders = riders[0] + riders[1]
    sources = [source.reshape((-1,) + source.shape[2:]) for source in sources]
    rows, cols, w1, w2, w2t = riders

    f32, bf16 = (jnp.float32, jnp.bfloat16)
    own, second = (plan.planes("own"), plan.planes("second"))
    second_x = plan.x["second"][1] - plan.x["second"][0]
    shape = jax.ShapeDtypeStruct
    near1, near2, slope1, slope2, delta, cot, stats, sums = pl.pallas_call(
        functools.partial(forward_kernel, plan, classes, scale),
        out_shape=[
            shape((plan.planes("near1"), 3 * chans, 128), bf16),
            shape((plan.planes("near2"), 3 * chans, 128), bf16),
            shape((own, chans, 128), f32),
            shape((second, chans, 128), f32),
            shape((2, second, chans, 128), bf16),
            shape((2, plan.planes("middle"), chans, 128), f32),
            shape((second, 8, 128), f32),
            shape((round_up(second_x * (1 + classes[2]), 8), 128), f32),
        ],
        in_specs=vmem(len(sources) + 4),
        out_specs=vmem(8),
        scratch_shapes=[
            pltpu.VMEM((plan.planes("input"), 3 * chans, 128), bf16),
            pltpu.VMEM((plan.planes("first"), 3 * chans, 128), bf16),
            pltpu.VMEM((plan.planes("first"), chans, 128), f32),
            pltpu.VMEM((plan.planes("input"), LABEL_ROWS, 128), f32),
        ],
        name="forward",
    )(*sources, w1, w2, rows, cols)

    sums = share_sums(sums, AXES if plan.whole else ("tile",))

    orders = [halving_order(0), halving_order(len(bits(tile_count)) // 2)]
    outs, scratch = backward_shapes(plan, 2)
    pair = pl.pallas_call(
        functools.partial(pair_kernel, plan, slots_of(plan, orders[0])),
        out_shape=outs,
        in_specs=vmem(6),
        out_specs=vmem(len(outs)),
        scratch_shapes=scratch,
        name="pair",
    )(delta, cot, slope1, near1, near2, w2t)
    if plan.aligned:
        pair = first_halving(*pair, orders[0])
    sums, *pair = lax.optimization_barrier((sums, *pair))
    outs, scratch = backward_shapes(plan, 1)
    scratch = [
        pltpu.VMEM((1, second, chans, 128), bf16),
        pltpu.VMEM((1, second, chans, 128), f32),
        pltpu.VMEM((1 + classes[2], chans, 128), f32),
    ] + scratch
    salt = pl.pallas_call(
        functools.partial(
            salt_kernel, plan, slots_of(plan, orders[1]), classes, plan.depth_total * scale
        ),
        out_shape=outs,
        in_specs=vmem(8),
        out_specs=vmem(len(outs)),
        scratch_shapes=scratch,
        name="salt",
    )(stats, sums, cols, slope2, slope1, near1, near2, w2t)

    terms = []
    if plan.aligned:
        salt = first_halving(*salt, orders[1])
        shared = reduce_shares([pair, salt], [order[1:] for order in orders])
        for share, tasks in zip(shared, (2, 1)):
            share = share[0, : plan.per_group * plan.pitch]
            share = share.reshape(plan.per_group, plan.pitch, -1)
            share = share[:, :27, : 2 * tasks * chans].reshape(-1, 2, tasks, chans)
            terms.append(share.transpose(1, 2, 0, 3).reshape(2, tasks, -1))
        grads = jnp.concatenate(terms, axis=1)
    else:
        for (value,), tasks in ((pair, 2), (salt, 1)):
            value = value[:, :27, : 2 * tasks * chans].reshape(chans, 27, 2, tasks, chans)
            terms.append(value.transpose(2, 3, 0, 1, 4).reshape(2, tasks, shares, -1))
        flat = jnp.concatenate(terms, axis=1).transpose(2, 0, 1, 3)
        left = [(axis, d) for axis in AXES for d in reversed(bits(lax.axis_size(axis)))]
        flat = flat.reshape((2,) * len(left) + flat.shape[1:])
        places = [left.index(entry) for entry in orders[0]]
        flat = flat.transpose(places + [len(left), len(left) + 1, len(left) + 2])
        flat = flat.reshape((-1,) + flat.shape[len(left) :])
        grads = reduce_shares([halve(flat, *orders[0][0])], orders[:1])[0][0]
    gram = jnp.sum(grads[:, :, None, :] * grads[:, None, :, :], axis=3)
    gram = share_sums(gram.reshape(2, 9), AXES).reshape(2, 3, 3) / (27 * chans * chans)
    return (grads, gram)


def solution(mesh):
    in_specs = (
        P(None, "inline", "tile", None),
        P(),
        P(),
        P(),
        P(),
        P(),
        P(),
        P("inline", "tile", None),
        P("inline", "tile", None),
        P("inline", None),
    )
    out_specs = (P(None, None, ("inline", "tile")), P())
    return jax.shard_map(
        on_device, mesh=mesh, in_specs=in_specs, out_specs=out_specs, check_vma=False
    )
```

```python
import functools
import math

import jax
import jax.numpy as jnp
from jax import lax
from jax.experimental import pallas as pl
from jax.experimental.pallas import tpu as pltpu
from jax.experimental.layout import Layout, with_layout_constraint
from jax.sharding import PartitionSpec as P


D1 = 1
D2 = 2
REACH = D1 + 2 * D2

CAPPING = 8.0
LABEL_ROWS = 8
AXES = ("inline", "tile")


def round_up(value, unit):
    return -(-value // unit) * unit


def bits(count):
    return [1 << bit for bit in range(count.bit_length() - 1)]


def swap_pairs(count, distance):
    return [(i, i ^ distance) for i in range(count)]


def window(cells, axis, dim, halo):
    count, length = (lax.axis_size(axis), cells.shape[dim])
    covered, hops = (0, 1)
    while covered < halo:
        amount = min(halo - covered, length + covered)
        size = cells.shape[dim]
        start = lax.slice_in_dim(cells, covered, covered + amount, axis=dim)
        end = lax.slice_in_dim(cells, size - covered - amount, size - covered, axis=dim)
        up = [(i, i + hops) for i in range(count - hops)]
        down = [(j, i) for i, j in up]
        before = lax.ppermute(end, axis, up)
        after = lax.ppermute(start, axis, down)
        cells = jnp.concatenate([before, cells, after], axis=dim)
        covered += amount
        hops = covered // length + 1
    return cells


def outward(cells, halo, needed, riders):
    ready = []
    here, length = (lax.axis_index("inline"), cells.shape[1])
    count = lax.axis_size("tile")
    chain = jnp.where(here == 0, cells[:, ::-1], cells)
    side = None
    covered, hops = (0, 1)
    while covered < halo:
        amount = min(halo - covered, length + covered)
        pairs = [(i, i + hops) for i in range(count - hops)]
        pairs += [(count + j, count + i) for i, j in pairs]
        taken = lax.ppermute(chain[:, :amount], AXES, pairs)
        if riders:
            taken, *made = lax.optimization_barrier((taken, *riders.pop(0)))
            ready += made
        side = taken if side is None else jnp.concatenate([side, taken], axis=1)
        chain = jnp.concatenate([chain, taken], axis=1)
        covered += amount
        hops = covered // length + 1
    for group in riders:
        ready += group
    other = lax.ppermute(side[:, :needed], "inline", [(0, 1), (1, 0)])
    return side, other, ready


def share_sums(value, axes):
    copies = jnp.broadcast_to(value, (lax.axis_size(axes),) + value.shape)
    return jnp.sum(lax.all_to_all(copies, axes, 0, 0), axis=0)


def halving_order(first):
    tile = bits(lax.axis_size("tile"))
    tile = tile[first : first + 1] + tile[:first] + tile[first + 1 :]
    inline = [("inline", distance) for distance in bits(lax.axis_size("inline"))]
    return inline + [("tile", distance) for distance in tile]


def halve(kept, axis, distance):
    half = kept.shape[0] // 2
    bit = (lax.axis_index(axis) // distance) % 2
    given = lax.dynamic_slice_in_dim(kept, (1 - bit) * half, half, 0).astype(jnp.bfloat16)
    return lax.dynamic_slice_in_dim(kept, bit * half, half, 0), given


def exchange(kept, given, axis, distance, after=None):
    taken = lax.ppermute(given, axis, swap_pairs(lax.axis_size(axis), distance))
    if after is not None:
        taken, _ = lax.optimization_barrier((taken, after))
    return kept + taken.astype(jnp.float32)


def first_halving(kept, given, order):
    kept = exchange(kept, given, *order[0])
    return halve(kept, *order[1])


def reduce_shares(chains, orders):
    chains, after = (list(chains), None)
    for step in range(max(len(order) for order in orders)):
        for n, order in enumerate(orders):
            if step >= len(order):
                continue
            kept = exchange(*chains[n], *order[step], after)
            last = step + 1 == len(order)
            chains[n] = (kept, None) if last else halve(kept, *order[step + 1])
            after = chains[n][1] if not last else after
    return [kept for kept, _ in chains]


class Plan:
    def __init__(self, inline_count, tile_count, inline_cells, depth_cells, chans, shares):
        self.inline_count, self.inline_cells = (inline_count, inline_cells)
        self.depth_cells = depth_cells
        self.inline_total = inline_count * inline_cells
        self.depth_total = tile_count * depth_cells
        self.chans = chans
        self.whole = inline_count == 2 and depth_cells % inline_count == 0
        self.own_depth = depth_cells // inline_count if self.whole else depth_cells
        own = range(self.own_depth)
        spread = lambda cells, d: sorted({z + d * b for z in cells for b in (-1, 0, 1)})
        self.z = {"own": list(own)}
        self.z["second"] = spread(self.z["own"], D2)
        self.z["first"] = spread(self.z["second"], D2)
        self.depth_width = depth_cells + 2 * REACH
        self.partner_reach = REACH
        self.z["near1"] = spread(self.z["own"], D1)
        self.z["near2"] = self.z["second"]
        self.z["middle"] = self.z["own"]
        reach = {"own": 0, "second": D2, "first": 2 * D2, "input": REACH, "near1": D1, "near2": D2}
        reach["middle"] = D2
        self.x = {}
        for name, halo in reach.items():
            if self.whole:
                self.x[name] = (0, self.inline_total)
            else:
                self.x[name] = (-halo, inline_cells + halo)
        self.aligned = chans % shares == 0 and inline_count % 2 == 0
        self.groups = shares if self.aligned else chans
        self.per_group = chans // self.groups
        self.pitch = 28 if self.aligned else 32
        self.rows = round_up(self.per_group * self.pitch, 8)
        self.half_rows = self.per_group * self.pitch // 2

    def pieces(self, tasks):
        lanes = 2 * tasks * self.chans
        chunks = list(range(-(-lanes // 128)))
        if tasks == 1:
            return [(chunks, len(chunks) > 1 and 0 < lanes % 128 <= 64 and self.aligned)]
        split = -(-2 * len(chunks) // 3)
        return [(part, False) for part in (chunks[:split], chunks[split:]) if part]

    def piece_shape(self, piece):
        chunks, folded = piece
        shares = self.groups // 2
        if folded:
            rows = (len(chunks) - 1) * self.rows + round_up(self.half_rows, 8)
            return (shares, rows, 128)
        return (shares, self.rows, 128 * len(chunks))

    def unpack(self, piece, share):
        chunks, folded = piece
        share, length = (share[0], self.per_group * self.pitch)
        if not folded:
            return share[:length]
        parts = [share[n * self.rows : n * self.rows + length] for n in range(len(chunks) - 1)]
        last = share[(len(chunks) - 1) * self.rows :][: self.half_rows]
        parts.append(jnp.concatenate([last[:, :64], last[:, 64:]], axis=0))
        return jnp.concatenate(parts, axis=1)

    def planes(self, name):
        low, high = self.x[name]
        return (high - low) * (self.depth_width if name == "input" else len(self.z[name]))

    def index(self, name, x, z):
        if name == "input":
            start = lax.axis_index("inline") * self.own_depth if self.whole else 0
            return (x - self.x[name][0]) * self.depth_width + z + start + REACH
        return (x - self.x[name][0]) * len(self.z[name]) + self.z[name].index(z)

    def runs(self, name, step):
        low, high = self.x[name]
        found = []
        for x in range(low, high):
            if self.whole:
                taps = tuple(a for a in (-1, 0, 1) if 0 <= x + step * a < self.inline_total)
            else:
                taps = (-1, 0, 1)
            if found and found[-1][0] == taps:
                found[-1][2] += 1
            else:
                found.append([taps, x, 1])
        return found


def depth_base(plan):
    start = lax.axis_index("tile") * plan.depth_cells
    if plan.whole:
        start = start + lax.axis_index("inline") * plan.own_depth
    return start


def inside(plan, x, z):
    depth = depth_base(plan) + z
    good = (depth >= 0) & (depth < plan.depth_total)
    if not plan.whole:
        cell = lax.axis_index("inline") * plan.inline_cells + x
        good = good & (cell >= 0) & (cell < plan.inline_total)
    return good


def each(count, body, unrolled=4):
    if count <= unrolled:
        for i in range(count):
            body(i)
    else:
        lax.fori_loop(0, count, lambda i, carry: (body(i), carry)[1], 0)


def shifted(plane, amount):
    if amount == 0:
        return plane
    width = plane.shape[1]
    column = lax.broadcasted_iota(jnp.int32, plane.shape, 1) + amount
    rolled = pltpu.roll(plane, (-amount) % width, 1)
    return jnp.where((column >= 0) & (column < width), rolled, 0.0)


def store_taps(ref, index, plane, offsets):
    chans = plane.shape[0]
    for place, amount in enumerate(offsets):
        ref[index, place * chans : (place + 1) * chans, :] = shifted(plane, amount).astype(
            jnp.bfloat16
        )


def sigmoid(value):
    return 1.0 / (1.0 + jnp.exp(-value))


def slope_of(value, sig):
    return sig * (1.0 + value * (1.0 - sig))


def matmul(left, right):
    return lax.dot_general(
        left, right, (((1,), (0,)), ((), ())), preferred_element_type=jnp.float32
    )


def matmul_nt(left, right):
    return lax.dot_general(
        left, right, (((1,), (1,)), ((), ())), preferred_element_type=jnp.float32
    )


def conv(weight_ref, taps, columns):
    total = None
    for a in taps:
        term = matmul(weight_ref[a + 1], columns(a))
        total = term if total is None else total + term
    return total


def joined(pieces, axis):
    return pieces[0] if len(pieces) == 1 else jnp.concatenate(pieces, axis=axis)


def softmax_cot(raw, expo, slope, label, scale):
    count = len(raw)
    total = expo[0]
    for n in range(1, count):
        total = total + expo[n]
    found = []
    for n in range(count):
        hit = jnp.where(label == float(n), 1.0, 0.0)
        found.append((expo[n] / total - hit) * slope[n] * scale)
    return found


def load_planes(plan, planes_refs, input_ref, marks_ref):
    chans = plan.chans

    def load(ref, i, to):
        plane = ref[i, :chans, :].astype(jnp.float32)
        store_taps(input_ref, to, plane, (-D1, 0, D1))
        marks_ref[to] = ref[i, chans : chans + LABEL_ROWS, :].astype(jnp.float32)

    if not plan.whole:
        (ref,) = planes_refs
        each(plan.planes("input"), lambda i: load(ref, i, i))
        return
    here = lax.axis_index("inline")
    width = plan.depth_width
    lower = lambda k: REACH - 1 - k
    upper = lambda k: REACH + plan.depth_cells + k
    for ref, fetcher, cells, place in (
        (planes_refs[0], here, plan.depth_cells, lambda k: REACH + k),
        (planes_refs[1], here, REACH, lambda k: jnp.where(here == 0, lower(k), upper(k))),
        (planes_refs[2], 1 - here, plan.partner_reach, lambda k: jnp.where(here == 0, upper(k), lower(k))),
    ):

        def row(i, ref=ref, fetcher=fetcher, cells=cells, place=place):
            x = lax.rem(i + fetcher * plan.inline_cells, plan.inline_total)
            for k in range(cells):
                load(ref, i * cells + k, x * width + place(k))

        each(plan.inline_total, row, 1)


def forward_kernel(plan, classes, scale, *refs):
    count = 3 if plan.whole else 1
    planes_refs, refs = (refs[:count], refs[count:])
    (
        w1_ref,
        w2_ref,
        rows_ref,
        cols_ref,
        near1_ref,
        near2_ref,
        slope1_ref,
        slope2_ref,
        delta_ref,
        cot_ref,
        stats_ref,
        sums_ref,
        input_ref,
        first_ref,
        base_ref,
        marks_ref,
    ) = refs
    chans = plan.chans
    faults, horizons, salts = classes
    zs = plan.z
    load_planes(plan, planes_refs, input_ref, marks_ref)

    for taps, begin, count in plan.runs("first", D1):

        def first(i, taps=taps, begin=begin):
            x = begin + i

            def columns(a):
                return joined(
                    [
                        joined(
                            [
                                input_ref[plan.index("input", x + D1 * a, z + D1 * b)]
                                for b in (-1, 0, 1)
                            ],
                            0,
                        )
                        for z in zs["first"]
                    ],
                    1,
                )

            pre = conv(w1_ref, taps, columns)
            for j, z in enumerate(zs["first"]):
                value = pre[:, j * 128 : (j + 1) * 128]
                field = input_ref[plan.index("input", x, z), chans : 2 * chans, :]
                sig = sigmoid(value)
                out = field.astype(jnp.float32) + value * sig
                out = out.astype(jnp.bfloat16).astype(jnp.float32)
                out = jnp.where(inside(plan, x, z), out, 0.0)
                store_taps(first_ref, plan.index("first", x, z), out, (-D2, 0, D2))
                if z in zs["own"]:
                    base_ref[plan.index("first", x, z)] = slope_of(value, sig)

        each(count, first)

    own_low, own_high = plan.x["own"]

    def keep_slope(i):
        x = own_low + i
        for z in zs["own"]:
            slope1_ref[plan.index("own", x, z)] = base_ref[plan.index("first", x, z)]

    each(own_high - own_low, keep_slope)

    for name, ref, source, source_ref in (
        ("near1", near1_ref, "input", input_ref),
        ("near2", near2_ref, "first", first_ref),
    ):
        near_low, near_high = plan.x[name]

        def keep(i, name=name, ref=ref, source=source, source_ref=source_ref, near_low=near_low):
            x = near_low + i
            for z in zs[name]:
                ref[plan.index(name, x, z)] = source_ref[plan.index(source, x, z)]

        each(near_high - near_low, keep)

    spread = [
        jnp.broadcast_to(cols_ref[:, n : n + 1], (chans, 128)) for n in range(faults + horizons)
    ]
    for n in range(faults + horizons):
        base_ref[n] = spread[n]

    used = (plan.x["second"][1] - plan.x["second"][0]) * (1 + salts)
    if used < sums_ref.shape[0]:
        sums_ref[used:, :] = jnp.zeros((sums_ref.shape[0] - used, 128), jnp.float32)

    for taps, begin, count in plan.runs("second", D2):

        def second(i, taps=taps, begin=begin):
            x = begin + i

            def columns(a):
                return joined(
                    [
                        joined(
                            [
                                first_ref[plan.index("first", x + D2 * a, z + D2 * b)]
                                for b in (-1, 0, 1)
                            ],
                            0,
                        )
                        for z in zs["second"]
                    ],
                    1,
                )

            pre = conv(w2_ref, taps, columns)
            field = joined(
                [
                    first_ref[plan.index("first", x, z), chans : 2 * chans, :]
                    for z in zs["second"]
                ],
                1,
            )
            sig = sigmoid(pre)
            slope2 = slope_of(pre, sig)
            second_out = (field.astype(jnp.float32) + pre * sig).astype(jnp.bfloat16)
            raw = matmul(rows_ref[...], second_out)
            squash = jnp.tanh(raw / CAPPING)
            expo = jnp.exp(CAPPING * squash)
            slope = 1.0 - squash * squash
            sums = None
            for j, z in enumerate(zs["second"]):
                lanes = slice(j * 128, (j + 1) * 128)
                row = lambda table, n: table[n : n + 1, lanes]
                marks = marks_ref[plan.index("input", x, z)]
                good = inside(plan, x, z)
                here = plan.index("second", x, z)
                slope2_ref[here] = slope2[:, lanes]
                for task, start, size in ((0, 0, faults), (1, faults, horizons)):
                    span = range(start, start + size)
                    dlog = softmax_cot(
                        [row(raw, n) for n in span],
                        [row(expo, n) for n in span],
                        [row(slope, n) for n in span],
                        marks[task : task + 1, :],
                        scale,
                    )
                    cot = None
                    for n, factor in zip(span, dlog):
                        term = base_ref[n] * factor
                        cot = term if cot is None else cot + term
                    if z in zs["own"]:
                        cot_ref[task, plan.index("middle", x, z)] = cot
                    delta = jnp.where(good, cot * slope2[:, lanes], 0.0)
                    delta_ref[task, here] = delta.astype(jnp.bfloat16)
                query = faults + horizons
                pieces = [row(expo, query)]
                pieces += [row(raw, query + 1 + n) for n in range(salts)]
                pieces += [row(slope, query), marks[2:3, :]]
                for n, piece in enumerate(pieces):
                    stats_ref[here, n : n + 1, :] = piece
                if z in zs["own"]:
                    terms = [pieces[0]] + [pieces[0] * piece for piece in pieces[1 : 1 + salts]]
                    if sums is None:
                        sums = terms
                    else:
                        sums = [old + new for old, new in zip(sums, terms)]
            place = x - plan.x["second"][0]
            for n, piece in enumerate(sums):
                sums_ref[pl.ds(place * (1 + salts) + n, 1), :] = piece

        each(count, second)


def salt_cotangents(plan, classes, scale, stats_ref, sums_ref, cols_ref, slope2_ref, delta_ref, cot_ref, spread_ref):
    faults, horizons, salts = classes
    chans = plan.chans
    query = faults + horizons
    for n in range(salts + 1):
        spread_ref[n] = jnp.broadcast_to(cols_ref[:, query + n : query + n + 1], (chans, 128))
    low, high = plan.x["second"]

    def one(i):
        x = low + i
        sums = [sums_ref[pl.ds(i * (1 + salts) + n, 1), :] for n in range(1 + salts)]
        total = sums[0]
        salt_raw = [value / total for value in sums[1:]]
        squash = [jnp.tanh(value / CAPPING) for value in salt_raw]
        label = stats_ref[plan.index("second", x, 0), salts + 2 : salts + 3, :]
        dlog = softmax_cot(
            salt_raw,
            [jnp.exp(CAPPING * value) for value in squash],
            [1.0 - value * value for value in squash],
            label,
            scale,
        )
        inner = dlog[0] * salt_raw[0]
        for n in range(1, salts):
            inner = inner + dlog[n] * salt_raw[n]
        for z in plan.z["second"]:
            here = plan.index("second", x, z)
            attn = stats_ref[here, 0:1, :] / total
            along = dlog[0] * stats_ref[here, 1:2, :]
            for n in range(1, salts):
                along = along + dlog[n] * stats_ref[here, 1 + n : 2 + n, :]
            dscore = attn * (along - inner) * stats_ref[here, salts + 1 : salts + 2, :]
            cot = spread_ref[0] * dscore
            for n in range(salts):
                cot = cot + spread_ref[1 + n] * (attn * dlog[n])
            cot_ref[0, here] = cot
            delta = jnp.where(inside(plan, x, z), cot * slope2_ref[here], 0.0)
            delta_ref[0, here] = delta.astype(jnp.bfloat16)

    each(high - low, one)


def backward_body(
    plan,
    tasks,
    delta_ref,
    cot_of,
    slope1_ref,
    near1_ref,
    near2_ref,
    w2t_ref,
    outs,
    taps_ref,
    first_delta_ref,
    second_delta_ref,
    rows_refs,
    slots,
):
    chans, zs = (plan.chans, plan.z)
    width = tasks * chans

    def spread(i):
        for task in range(tasks):
            plane = delta_ref[task, i].astype(jnp.float32)
            store_taps(taps_ref, task * plan.planes("second") + i, plane, (D2, 0, -D2))

    each(plan.planes("second"), spread)

    for taps, begin, count in plan.runs("own", -D2):

        def back(i, taps=taps, begin=begin):
            x = begin + i

            def columns(a):
                return joined(
                    [
                        joined(
                            [
                                taps_ref[
                                    task * plan.planes("second")
                                    + plan.index("second", x - D2 * a, z - D2 * b)
                                ]
                                for b in (-1, 0, 1)
                            ],
                            0,
                        )
                        for task in range(tasks)
                        for z in zs["own"]
                    ],
                    1,
                )

            pulled = conv(w2t_ref, taps, columns)
            column = 0
            for task in range(tasks):
                for z in zs["own"]:
                    here = plan.index("own", x, z)
                    cot = cot_of(task, x, z) + pulled[:, column * 128 : (column + 1) * 128]
                    place = slice(task * chans, (task + 1) * chans)
                    first_delta_ref[here, place, :] = (cot * slope1_ref[here]).astype(jnp.bfloat16)
                    second_delta_ref[here, place, :] = delta_ref[task, plan.index("second", x, z)]
                    column += 1

        each(count, back)

    own_low, own_high = plan.x["own"]
    lanes = 128
    for ref in rows_refs:
        ref[chans * plan.pitch :, :] = jnp.zeros((8, lanes), jnp.float32)
    for tap in range(27, plan.pitch):
        for ref in rows_refs:
            ref[pl.ds(tap, chans, stride=plan.pitch), :] = jnp.zeros((chans, lanes), jnp.float32)
    for a in (-1, 0, 1):
        for b in (-1, 0, 1):
            chunks = {}
            for ref, name, d, delta_own, begin in (
                (near1_ref, "near1", D1, first_delta_ref, 0),
                (near2_ref, "near2", D2, second_delta_ref, width),
            ):
                cells = []
                for x in range(own_low, own_high):
                    if plan.whole and not 0 <= x + d * a < plan.inline_total:
                        continue
                    cells += [(x, z) for z in zs["own"]]
                left = joined([ref[plan.index(name, x + d * a, z + d * b)] for x, z in cells], 1)
                right = joined([delta_own[plan.index("own", x, z)] for x, z in cells], 1)
                before = begin % lanes
                after = -(before + width) % lanes
                parts = [right]
                if before:
                    parts = [jnp.zeros((before, right.shape[1]), right.dtype)] + parts
                if after:
                    parts = parts + [jnp.zeros((after, right.shape[1]), right.dtype)]
                grad = matmul_nt(left, joined(parts, 0))
                for n in range(grad.shape[1] // lanes):
                    chunk = begin // lanes + n
                    piece = grad[:, n * lanes : (n + 1) * lanes]
                    chunks[chunk] = chunks[chunk] + piece if chunk in chunks else piece
            for chunk, value in chunks.items():
                for c in range(3):
                    tap = 9 * (a + 1) + 3 * (b + 1) + c
                    rows_refs[chunk][pl.ds(tap, chans, stride=plan.pitch), :] = value[
                        c * chans : (c + 1) * chans, :
                    ]
    if plan.aligned:
        half = lax.rem(lax.axis_index("inline"), 2)
        tiles = plan.groups // plan.inline_count
        length = plan.per_group * plan.pitch
        lane = lax.broadcasted_iota(jnp.int32, (round_up(plan.half_rows, 8), lanes), 1)

        def share_of(ref, bit, high, j, start, count):
            base = pl.multiple_of((2 * high + bit) * tiles * length, 8)
            block = ref.at[pl.ds(base, tiles * length + 8), :]
            return block[j * length + start : j * length + start + count, :]

        for number, (chunks, folded) in enumerate(plan.pieces(tasks)):
            for target_ref, bit in ((outs[2 * number], half), (outs[2 * number + 1], 1 - half)):
                kind = target_ref.dtype
                for high in range(plan.inline_count // 2):
                    for j in range(tiles):
                        slot = slots[number][high * tiles + j]
                        for place, chunk in enumerate(chunks):
                            ref = rows_refs[chunk]
                            if folded and place == len(chunks) - 1:
                                count = lane.shape[0]
                                left = share_of(ref, bit, high, j, 0, count)
                                right = share_of(ref, bit, high, j, plan.half_rows, count)
                                value = jnp.where(lane < 64, left, pltpu.roll(right, 64, 1))
                                span = slice(place * plan.rows, place * plan.rows + count)
                                target_ref[slot, span, :] = value.astype(kind)
                                continue
                            value = share_of(ref, bit, high, j, 0, plan.rows).astype(kind)
                            if folded:
                                span = slice(place * plan.rows, (place + 1) * plan.rows)
                                target_ref[slot, span, :] = value
                            else:
                                span = slice(place * lanes, (place + 1) * lanes)
                                target_ref[slot, :, span] = value
    else:
        (out_ref,) = outs

        def write(j):
            for chunk, ref in enumerate(rows_refs):
                start = pl.multiple_of(j * plan.pitch, 8)
                span = slice(chunk * lanes, (chunk + 1) * lanes)
                out_ref[j, :, span] = ref[pl.ds(start, plan.pitch), :]

        each(plan.groups, write)


def pair_kernel(
    plan, slots, delta_ref, cot_ref, slope1_ref, near1_ref, near2_ref, w2t_ref, *rest
):
    outs, scratch = split_refs(plan, 2, rest)
    cot_of = lambda task, x, z: cot_ref[task, plan.index("middle", x, z)]
    backward_body(
        plan,
        2,
        delta_ref,
        cot_of,
        slope1_ref,
        near1_ref,
        near2_ref,
        w2t_ref,
        outs,
        *scratch[:3],
        scratch[3:],
        slots,
    )


def salt_kernel(
    plan,
    slots,
    classes,
    scale,
    stats_ref,
    sums_ref,
    cols_ref,
    slope2_ref,
    slope1_ref,
    near1_ref,
    near2_ref,
    w2t_ref,
    *rest,
):
    outs, scratch = split_refs(plan, 1, rest)
    delta_ref, cot_ref, spread_ref = scratch[:3]
    salt_cotangents(
        plan,
        classes,
        scale,
        stats_ref,
        sums_ref,
        cols_ref,
        slope2_ref,
        delta_ref,
        cot_ref,
        spread_ref,
    )
    cot_of = lambda task, x, z: cot_ref[task, plan.index("second", x, z)]
    backward_body(
        plan,
        1,
        delta_ref,
        cot_of,
        slope1_ref,
        near1_ref,
        near2_ref,
        w2t_ref,
        outs,
        *scratch[3:6],
        scratch[6:],
        slots,
    )


def split_refs(plan, tasks, refs):
    count = 2 * len(plan.pieces(tasks)) if plan.aligned else 1
    return (refs[:count], refs[count:])


def vmem(count):
    return [pl.BlockSpec(memory_space=pltpu.VMEM)] * count


def backward_shapes(plan, tasks):
    chans = plan.chans
    width = round_up(2 * tasks * chans, 128)
    if plan.aligned:
        outs = []
        for piece in plan.pieces(tasks):
            for kind in (jnp.float32, jnp.bfloat16):
                outs.append(jax.ShapeDtypeStruct(plan.piece_shape(piece), kind))
    else:
        outs = [jax.ShapeDtypeStruct((plan.groups, plan.pitch, width), jnp.float32)]
    scratch = [
        pltpu.VMEM((tasks * plan.planes("second"), 3 * chans, 128), jnp.bfloat16),
        pltpu.VMEM((plan.planes("own"), tasks * chans, 128), jnp.bfloat16),
        pltpu.VMEM((plan.planes("own"), tasks * chans, 128), jnp.bfloat16),
    ]
    scratch += [pltpu.VMEM((chans * plan.pitch + 8, 128), jnp.float32)] * (width // 128)
    return (outs, scratch)


def tap_major(weight, flip):
    ins, _, outs = weight.shape
    parts = weight.reshape(ins, 3, 9, outs)
    if flip:
        parts = parts.transpose(1, 0, 2, 3).reshape(3, ins, 9 * outs)
    else:
        parts = parts.transpose(1, 3, 2, 0).reshape(3, outs, 9 * ins)
    return with_layout_constraint(parts, Layout(major_to_minor=(0, 1, 2)))


def slots_of(plan, order):
    if not plan.aligned:
        return None
    tiles = plan.groups // plan.inline_count
    slots = []
    for high in range(plan.inline_count // 2):
        for tile in range(tiles):
            slot = 0
            for axis, distance in order[1:]:
                index = 2 * high if axis == "inline" else tile
                slot = 2 * slot + index // distance % 2
            slots.append(slot)
    return slots


def on_device(
    features,
    conv1_weight,
    conv2_weight,
    fault_head,
    horizon_head,
    salt_query,
    salt_head,
    fault_labels,
    horizon_labels,
    salt_labels,
):
    chans, inline_cells, depth_cells, cross_cells = features.shape
    inline_count, tile_count = (lax.axis_size("inline"), lax.axis_size("tile"))
    shares = inline_count * tile_count
    plan = Plan(inline_count, tile_count, inline_cells, depth_cells, chans, shares)
    scale = 1.0 / math.sqrt(plan.inline_total * plan.depth_total * cross_cells)
    classes = (fault_head.shape[1], horizon_head.shape[1], salt_head.shape[1])

    marks = jnp.stack(
        [
            fault_labels,
            horizon_labels,
            jnp.broadcast_to(salt_labels[:, None, :], fault_labels.shape),
        ],
        axis=2,
    ).astype(jnp.bfloat16)
    marks = jnp.pad(marks, ((0, 0), (0, 0), (0, LABEL_ROWS - 3), (0, 0)))
    planes = jnp.concatenate([features.transpose(1, 2, 0, 3), marks], axis=2)
    cols = jnp.concatenate([fault_head, horizon_head, salt_query[:, None], salt_head], axis=1)
    cols = jnp.pad(cols, ((0, 0), (0, 16 - cols.shape[1])))
    riders = [
        [cols.T, cols.astype(jnp.float32), tap_major(conv1_weight, False)],
        [tap_major(conv2_weight, False), tap_major(conv2_weight, True)],
    ]
    if plan.whole:
        other = lax.ppermute(planes, "inline", [(0, 1), (1, 0)])
        planes = jnp.concatenate([planes, other], axis=0)
        mine, theirs, riders = outward(planes, REACH, plan.partner_reach, riders)
        sources = [planes, mine, theirs]
    else:
        planes = window(planes, "tile", 1, REACH)
        sources = [window(planes, "inline", 0, REACH)]
        riders = riders[0] + riders[1]
    sources = [source.reshape((-1,) + source.shape[2:]) for source in sources]
    rows, cols, w1, w2, w2t = riders

    f32, bf16 = (jnp.float32, jnp.bfloat16)
    own, second = (plan.planes("own"), plan.planes("second"))
    second_x = plan.x["second"][1] - plan.x["second"][0]
    shape = jax.ShapeDtypeStruct
    near1, near2, slope1, slope2, delta, cot, stats, sums = pl.pallas_call(
        functools.partial(forward_kernel, plan, classes, scale),
        out_shape=[
            shape((plan.planes("near1"), 3 * chans, 128), bf16),
            shape((plan.planes("near2"), 3 * chans, 128), bf16),
            shape((own, chans, 128), f32),
            shape((second, chans, 128), f32),
            shape((2, second, chans, 128), bf16),
            shape((2, plan.planes("middle"), chans, 128), f32),
            shape((second, 8, 128), f32),
            shape((round_up(second_x * (1 + classes[2]), 8), 128), f32),
        ],
        in_specs=vmem(len(sources) + 4),
        out_specs=vmem(8),
        scratch_shapes=[
            pltpu.VMEM((plan.planes("input"), 3 * chans, 128), bf16),
            pltpu.VMEM((plan.planes("first"), 3 * chans, 128), bf16),
            pltpu.VMEM((plan.planes("first"), chans, 128), f32),
            pltpu.VMEM((plan.planes("input"), LABEL_ROWS, 128), f32),
        ],
        name="forward",
    )(*sources, w1, w2, rows, cols)

    sums = share_sums(sums, AXES if plan.whole else ("tile",))

    order_of = {0: halving_order(0), 1: halving_order(1), 2: halving_order(2)}
    pair_slots = [slots_of(plan, order_of[n]) for n in range(len(plan.pieces(2)))]
    outs, scratch = backward_shapes(plan, 2)
    pair = pl.pallas_call(
        functools.partial(pair_kernel, plan, pair_slots),
        out_shape=outs,
        in_specs=vmem(6),
        out_specs=vmem(len(outs)),
        scratch_shapes=scratch,
        name="pair",
    )(delta, cot, slope1, near1, near2, w2t)
    pair = list(pair)
    if plan.aligned:
        for n in range(len(pair) // 2):
            pair[2 * n : 2 * n + 2] = first_halving(pair[2 * n], pair[2 * n + 1], order_of[n])
    sums, *pair = lax.optimization_barrier((sums, *pair))
    outs, scratch = backward_shapes(plan, 1)
    scratch = [
        pltpu.VMEM((1, second, chans, 128), bf16),
        pltpu.VMEM((1, second, chans, 128), f32),
        pltpu.VMEM((1 + classes[2], chans, 128), f32),
    ] + scratch
    operands = (stats, sums, cols, slope2, slope1, near1, near2, w2t)
    held = sum(
        math.prod(ref.shape) * jnp.dtype(ref.dtype).itemsize
        for ref in [*operands, *outs, *scratch]
    )
    salt_limit = max(24 << 20, 2 * held)
    salt = pl.pallas_call(
        functools.partial(
            salt_kernel, plan, [slots_of(plan, order_of[2])], classes, plan.depth_total * scale
        ),
        out_shape=outs,
        in_specs=vmem(8),
        out_specs=vmem(len(outs)),
        scratch_shapes=scratch,
        compiler_params=pltpu.CompilerParams(vmem_limit_bytes=salt_limit),
        name="salt",
    )(*operands)

    terms = []
    if plan.aligned:
        chains = [pair[-2:], salt] + ([pair[:2]] if len(pair) > 2 else [])
        orders = [order_of[len(pair) // 2 - 1][1:], order_of[2], order_of[0][1:]][: len(chains)]
        shares_of = reduce_shares(chains, orders)
        pair = [plan.unpack(*each) for each in zip(plan.pieces(2), shares_of[2:] + shares_of[:1])]
        salt = plan.unpack(plan.pieces(1)[0], shares_of[1])
        for share, tasks in ((joined(pair, 1), 2), (salt, 1)):
            share = share.reshape(plan.per_group, plan.pitch, -1)
            share = share[:, :27, : 2 * tasks * chans].reshape(-1, 2, tasks, chans)
            terms.append(share.transpose(1, 2, 0, 3).reshape(2, tasks, -1))
        grads = jnp.concatenate(terms, axis=1)
    else:
        for (value,), tasks in ((pair, 2), (salt, 1)):
            value = value[:, :27, : 2 * tasks * chans].reshape(chans, 27, 2, tasks, chans)
            terms.append(value.transpose(2, 3, 0, 1, 4).reshape(2, tasks, shares, -1))
        flat = jnp.concatenate(terms, axis=1).transpose(2, 0, 1, 3)
        left = [(axis, d) for axis in AXES for d in reversed(bits(lax.axis_size(axis)))]
        flat = flat.reshape((2,) * len(left) + flat.shape[1:])
        places = [left.index(entry) for entry in order_of[0]]
        flat = flat.transpose(places + [len(left), len(left) + 1, len(left) + 2])
        flat = flat.reshape((-1,) + flat.shape[len(left) :])
        grads = reduce_shares([halve(flat, *order_of[0][0])], [order_of[0]])[0][0]
    gram = jnp.sum(grads[:, :, None, :] * grads[:, None, :, :], axis=3)
    gram = share_sums(gram.reshape(2, 9), AXES).reshape(2, 3, 3) / (27 * chans * chans)
    return (grads, gram)


def solution(mesh):
    in_specs = (
        P(None, "inline", "tile", None),
        P(),
        P(),
        P(),
        P(),
        P(),
        P(),
        P("inline", "tile", None),
        P("inline", "tile", None),
        P("inline", None),
    )
    out_specs = (P(None, None, ("inline", "tile")), P())
    return jax.shard_map(
        on_device, mesh=mesh, in_specs=in_specs, out_specs=out_specs, check_vma=False
    )
```
